128 devices in a mesh: row: 16 (over y, x), col: 4 (over z), dp: 2 (over core).
Axes of the slice: x: 4, y: 4, z: 4, core: 2. Of those that a mesh axis runs over, the one named last changes fastest.
Arguments:
- inputs: bfloat16 [1024, 8192], P(('col', 'dp'), 'row'), may hold values from -6 to 6
- gate_weight: bfloat16 [8192, 14336], P('row', 'col'), may hold values from -0.0625 to 0.0625
- up_weight: bfloat16 [8192, 14336], P('row', 'col'), may hold values from -0.0625 to 0.0625
- down_weight: bfloat16 [14336, 8192], P('col', 'row'), may hold values from -0.046875 to 0.046875
- reward_head: bfloat16 [8192], P('row'), may hold values from -0.0625 to 0.0625
- upstream: bfloat16 [1024, 8192], P(('col', 'dp'), 'row'), may hold values from -0.59765625 to 0.59765625
- labels: int32 [1024], P(('col', 'dp')), may hold values from 0 to 1
- label_mask: int32 [1024], P(('col', 'dp')), may hold values 0 or 1
Outputs:
- gate_grad: float32 [8192, 14336], P(('row', 'dp'), 'col')
- up_grad: float32 [8192, 14336], P(('row', 'dp'), 'col')
- down_grad: float32 [14336, 8192], P(('col', 'dp'), 'row')
- input_grad: float32 [1024, 8192], P(('col', 'dp'), 'row')
The draws below stay inside these ranges and needn't reach their ends.
All inputs are finite; a program needn't handle non-finite values. No bound on the sum of `label_mask` on one device may be relied on, other than what follows from the above.
Results may differ from the reference program's by a relative error of at most 0.035.
Values may be sent and summed in bfloat16 or wider, within the bound.
No kernel may reach another device: no remote copies, remote signals or barrier semaphores. Data moves between devices by JAX's collectives and lax.ppermute only.
A program may use at most 128 MiB of HBM per device.

```python
import jax
import jax.numpy as jnp
from jax import lax

D = 8192
FF = 14336
TOK_DEV = 128
TOKENS = 1024
N_ROW = 16
N_COL = 4
N_DP = 2


def set_ends(entries, key, low, high):
    spot = [jax.random.randint(jax.random.fold_in(key, axis), (), 0, length) for axis, length in enumerate(entries.shape)]
    main_axis = entries.shape.index(max(entries.shape))
    beside = spot[:main_axis] + [(spot[main_axis] + 1) % entries.shape[main_axis]] + spot[main_axis + 1:]
    return entries.at[tuple(spot)].set(low).at[tuple(beside)].set(high)


def level_of(rng, dims, shards, low, high):
    def one(position, shards_of):
        steps = jax.random.uniform(jax.random.fold_in(jax.random.fold_in(rng, 6), position), (shards_of,), jnp.float32, low / len(shards), high / len(shards))
        return jnp.repeat(jnp.exp(steps), dims[position] // shards_of).reshape((-1,) + (1,) * (len(dims) - position - 1))

    factor_of = one(*shards[0])
    for cut in shards[1:]:
        factor_of = factor_of * one(*cut)
    return factor_of


def scatter_about(key, dims, deviation, limit, cuts=(), held_as=jnp.bfloat16):
    result = deviation * jax.random.normal(key, dims, jnp.float32)
    if cuts:
        result = result * level_of(key, dims, cuts, -0.22, 0.18)
    return jnp.clip(result, -limit, limit).astype(held_as)


def setup_inputs(seed: int = 0) -> dict:
    splits = jax.random.split(jax.random.key(seed), 9)
    inputs = scatter_about(splits[0], (TOKENS, D), 1.0, 6.0, ((0, 8), (1, 16)))
    gate_weight = scatter_about(splits[1], (D, FF), D ** -0.5, 0.0625, ((0, 16), (1, 4)))
    up_weight = scatter_about(splits[2], (D, FF), D ** -0.5, 0.0625, ((0, 16), (1, 4)))
    down_weight = scatter_about(splits[3], (FF, D), FF ** -0.5, 0.046875, ((0, 4), (1, 16)))
    reward_head = scatter_about(splits[4], (D,), D ** -0.5, 0.0625, ((0, 16),))
    upstream = scatter_about(splits[5], (TOKENS, D), 0.1, 0.59765625, ((0, 8), (1, 16)))
    labels = set_ends(jax.random.randint(splits[6], (TOKENS,), 0, 2), jax.random.fold_in(splits[6], 1), 0, 1).astype(jnp.int32)
    label_mask = set_ends((jax.random.randint(splits[7], (TOKENS,), 0, 2) < 1).astype(jnp.int32), jax.random.fold_in(splits[7], 1), 0, 1)
    return dict(inputs=inputs, gate_weight=gate_weight, up_weight=up_weight, down_weight=down_weight, reward_head=reward_head, upstream=upstream, labels=labels, label_mask=label_mask)


def rounded(value):
    return lax.optimization_barrier(value.astype(jnp.bfloat16)).astype(jnp.float32)


def transpose_product(left, right):
    return lax.dot_general(left, right, (((0,), (0,)), ((), ())), preferred_element_type=jnp.float32)


def right_transpose(left, right):
    return lax.dot_general(left, right, (((1,), (1,)), ((), ())), preferred_element_type=jnp.float32)


def replica_rows(array, replica):
    return array.reshape(N_COL, N_DP, TOK_DEV, array.shape[-1])[:, replica].reshape(-1, array.shape[-1])


def reference(inputs, gate_weight, up_weight, down_weight, reward_head, upstream, labels, label_mask):
    span = D // N_ROW
    gate = jnp.zeros((TOKENS, FF), jnp.float32)
    upper = jnp.zeros((TOKENS, FF), jnp.float32)
    for block in range(N_ROW):
        cols = inputs[:, block * span:(block + 1) * span]
        gate = gate + rounded(jnp.dot(cols, gate_weight[block * span:(block + 1) * span], preferred_element_type=jnp.float32))
        upper = upper + rounded(jnp.dot(cols, up_weight[block * span:(block + 1) * span], preferred_element_type=jnp.float32))
    sig = jax.nn.sigmoid(gate)
    hidden = (gate * sig * upper).astype(jnp.bfloat16)
    outcome = inputs.astype(jnp.float32) + jnp.dot(hidden, down_weight, preferred_element_type=jnp.float32)
    head_value = reward_head.astype(jnp.float32)
    score = jnp.dot(outcome, head_value, precision=lax.Precision.HIGHEST)
    slope = 8.0 * label_mask.astype(jnp.float32) * (jax.nn.sigmoid(score) - labels.astype(jnp.float32))
    grad_out = upstream.astype(jnp.float32) + slope[:, None] * head_value[None, :]
    grad_mixed = grad_out.astype(jnp.bfloat16)
    grad_hidden = right_transpose(grad_mixed, down_weight)
    grad_gate = (grad_hidden * upper * sig * (1.0 + gate * (1.0 - sig))).astype(jnp.bfloat16)
    grad_upper = (grad_hidden * gate * sig).astype(jnp.bfloat16)
    input_grad = grad_out + right_transpose(grad_gate, gate_weight) + right_transpose(grad_upper, up_weight)
    gate_grad = jnp.zeros((D, FF), jnp.float32)
    up_grad = jnp.zeros((D, FF), jnp.float32)
    down_grad = jnp.zeros((FF, D), jnp.float32)
    for replica in range(N_DP):
        x_part = replica_rows(inputs, replica)
        gate_grad = gate_grad + rounded(transpose_product(x_part, replica_rows(grad_gate, replica)))
        up_grad = up_grad + rounded(transpose_product(x_part, replica_rows(grad_upper, replica)))
        down_grad = down_grad + rounded(transpose_product(replica_rows(hidden, replica), replica_rows(grad_mixed, replica)))
    return gate_grad, up_grad, down_grad, input_grad
```

```python
import jax
import jax.numpy as jnp
from jax import lax
from jax.sharding import PartitionSpec as P

reward_weight = 8.0
BF = jnp.bfloat16
F32 = jnp.float32


def transpose_product(left, right):
    return lax.dot_general(
        left, right, (((0,), (0,)), ((), ())), preferred_element_type=F32
    )


def right_transpose(left, right):
    return lax.dot_general(
        left, right, (((1,), (1,)), ((), ())), preferred_element_type=F32
    )


def per_device(
    inputs, gate_weight, up_weight, down_weight, reward_head, upstream, labels, label_mask
):
    tokens, depth = inputs.shape
    half = gate_weight.shape[1] // 2
    n_row = lax.axis_size("row")
    core = lax.axis_index("dp")
    row = lax.axis_index("row")
    token_axes = ("col", "dp")

    tags = jnp.stack([labels, label_mask], axis=1).astype(BF)
    tags = jnp.pad(tags, ((0, 0), (0, 126)))
    packed = jnp.concatenate([inputs, upstream, tags], axis=1)
    everyone = lax.all_gather(packed, token_axes, axis=0, tiled=True)
    x_all = everyone[:, :depth]
    upstream_all = everyone[:, depth : 2 * depth]
    total = x_all.shape[0]
    mine = total // n_row

    gate_half = lax.dynamic_slice_in_dim(gate_weight, core * half, half, 1)
    up_half = lax.dynamic_slice_in_dim(up_weight, core * half, half, 1)
    down_half = lax.dynamic_slice_in_dim(down_weight, core * half, half, 0)
    head_value = reward_head.astype(F32)

    head_hidden = jnp.dot(down_half.astype(F32), head_value, precision=lax.Precision.HIGHEST)
    head_inputs = jnp.dot(x_all.astype(F32), head_value, precision=lax.Precision.HIGHEST)
    per_token = half // mine
    extras = jnp.concatenate(
        [
            head_inputs[:, None],
            jnp.tile(head_hidden.reshape(mine, per_token), (n_row, 1)),
            jnp.zeros((total, 127 - per_token), F32),
        ],
        axis=1,
    )
    partial = jnp.concatenate(
        [
            jnp.dot(x_all, gate_half, preferred_element_type=F32).astype(BF),
            jnp.dot(x_all, up_half, preferred_element_type=F32).astype(BF),
            right_transpose(upstream_all, down_half).astype(BF),
            extras.astype(BF),
        ],
        axis=1,
    )
    summed = lax.psum_scatter(partial, "row", scatter_dimension=0, tiled=True).astype(F32)
    gate = summed[:, :half]
    upper = summed[:, half : 2 * half]
    grad_upstream = summed[:, 2 * half : 3 * half]
    extra = summed[:, 3 * half :]
    head_hidden = extra[:, 1 : 1 + per_token].reshape(half)

    sigmoid_gate = jax.nn.sigmoid(gate)
    hidden = (gate * sigmoid_gate * upper).astype(BF)
    score = extra[:, 0] + lax.psum(
        jnp.sum(hidden.astype(F32) * head_hidden[None, :], axis=1), token_axes
    )
    own_tags = lax.dynamic_slice_in_dim(everyone[:, 2 * depth :], row * mine, mine, 0).astype(F32)
    slope = reward_weight * own_tags[:, 1] * (jax.nn.sigmoid(score) - own_tags[:, 0])
    grad_hidden = grad_upstream + slope[:, None] * head_hidden[None, :]
    grad_gate = (grad_hidden * upper * sigmoid_gate * (1.0 + gate * (1.0 - sigmoid_gate))).astype(
        BF
    )
    grad_upper = (grad_hidden * gate * sigmoid_gate).astype(BF)
    slope_high = slope.astype(BF)
    slope_low = (slope - slope_high.astype(F32)).astype(BF)
    slopes = jnp.pad(jnp.stack([slope_high, slope_low], axis=1), ((0, 0), (0, 126)))
    gathered = lax.all_gather(
        jnp.concatenate([hidden, grad_gate, grad_upper, slopes], axis=1), "row", axis=0, tiled=True
    )
    hidden_all = gathered[:, :half]
    grad_gate_all = gathered[:, half : 2 * half]
    grad_upper_all = gathered[:, 2 * half : 3 * half]
    slope_all = gathered[:, 3 * half].astype(F32) + gathered[:, 3 * half + 1].astype(F32)

    input_part = right_transpose(grad_gate_all, gate_half) + right_transpose(
        grad_upper_all, up_half
    )
    input_sum = lax.psum_scatter(
        input_part.astype(BF), token_axes, scatter_dimension=0, tiled=True
    ).astype(F32)
    place = (lax.axis_index("col") * 2 + core) * tokens
    own_slope = lax.dynamic_slice_in_dim(slope_all, place, tokens, 0)
    input_grad = (
        upstream.astype(F32) + own_slope[:, None] * head_value[None, :] + input_sum
    )

    grad_mixed = (
        upstream_all.astype(F32) + slope_all[:, None] * head_value[None, :]
    ).astype(BF)
    down_grad = transpose_product(hidden_all, grad_mixed)

    def both_halves(part):
        keep = lax.dynamic_slice_in_dim(part, core * (depth // 2), depth // 2, 0)
        send = lax.dynamic_slice_in_dim(part, (1 - core) * (depth // 2), depth // 2, 0)
        other = lax.ppermute(send.astype(BF), "dp", [(0, 1), (1, 0)]).astype(F32)
        first = core == 0
        return jnp.concatenate(
            [jnp.where(first, keep, other), jnp.where(first, other, keep)], axis=1
        )

    gate_grad = both_halves(transpose_product(x_all, grad_gate_all))
    up_grad = both_halves(transpose_product(x_all, grad_upper_all))
    return (gate_grad, up_grad, down_grad, input_grad)


def solution(mesh):
    in_specs = (
        P(("col", "dp"), "row"),
        P("row", "col"),
        P("row", "col"),
        P("col", "row"),
        P("row"),
        P(("col", "dp"), "row"),
        P(("col", "dp")),
        P(("col", "dp")),
    )
    out_specs = (
        P(("row", "dp"), "col"),
        P(("row", "dp"), "col"),
        P(("col", "dp"), "row"),
        P(("col", "dp"), "row"),
    )
    return jax.shard_map(
        per_device, mesh=mesh, in_specs=in_specs, out_specs=out_specs, check_vma=False
    )
```

```python
import jax
import jax.numpy as jnp
from jax import lax
from jax.experimental import pallas as pl
from jax.experimental.pallas import tpu as pltpu
from jax.sharding import PartitionSpec as P

reward_weight = 8.0
BF = jnp.bfloat16
F32 = jnp.float32
AXES = ("row", "col", "dp")
SIDE = 4


def transpose_product(left, right):
    return lax.dot_general(
        left, right, (((0,), (0,)), ((), ())), preferred_element_type=F32
    )


def right_transpose(left, right):
    return lax.dot_general(
        left, right, (((1,), (1,)), ((), ())), preferred_element_type=F32
    )


def product(left, right):
    return jnp.dot(left, right, preferred_element_type=F32)


def flat(y, x, z, c):
    return ((y * SIDE + x) * 4 + z) * 2 + c


def pairs(move):
    found = []
    for y in range(SIDE):
        for x in range(SIDE):
            for z in range(4):
                for c in range(2):
                    found.append((flat(y, x, z, c), flat(*move(y, x, z, c))))
    return found


def step_first(s):
    return pairs(
        lambda y, x, z, c: (y, (x + s) % SIDE, z, c) if c == 0 else ((y + s) % SIDE, x, z, c)
    )


def step_second(s):
    return pairs(
        lambda y, x, z, c: ((y + s) % SIDE, x, z, c) if c == 0 else (y, (x + s) % SIDE, z, c)
    )


FIRST = {s: step_first(s) for s in (1, 2, 3)}
SECOND = {s: step_second(s) for s in (1, 2, 3)}
TWIN = pairs(lambda y, x, z, c: (x, y, z, 1 - c))


def move(value, links):
    return lax.ppermute(value, AXES, links)


AHEAD = {s: pairs(lambda y, x, z, c, s=s: (y, x, (z + s) % 4, c)) for s in (1, 2, 3)}
OTHER = pairs(lambda y, x, z, c: (y, x, z, 1 - c))


def together(*values):
    return lax.optimization_barrier(values)


def parts_of(value, n):
    found = []
    for _ in range(n):
        found.append(value.astype(BF))
        value = value - found[-1].astype(F32)
    return found


def params(mib=50):
    return pltpu.CompilerParams(vmem_limit_bytes=mib << 20)


def project(core, x_all, u_all, weights, heads, far):
    total, depth = x_all.shape
    tile = weights[0].shape[1] // 4
    n = total // 4
    h = n // 2
    spread = heads[1].shape[0]
    starts = (0, h) if far else (n + h, 3 * n, n, 3 * n + h, 0, h)
    types = (BF, BF) if far else (BF, BF, F32, F32, F32, F32)

    def kernel(core_ref, x_ref, u_ref, gate_ref, up_ref, down_ref, head_ref, spread_ref, *outs):
        step = pl.program_id(0)

        def run(rows_ref, of):
            for start, out in zip(starts, outs):
                value = of(rows_ref[start : start + h])
                out[:, : value.shape[1]] = value.astype(out.dtype)

        def heads_of(rows):
            return product(rows, head_ref[...]) + jnp.concatenate(
                [spread_ref[...]] * (h // spread), 0
            )

        pl.when(step < 2)(lambda: run(x_ref, lambda rows: product(rows, gate_ref[...])))
        pl.when((step >= 2) & (step < 4))(
            lambda: run(x_ref, lambda rows: product(rows, up_ref[...]))
        )
        pl.when((step >= 4) & (step < 6))(
            lambda: run(u_ref, lambda rows: right_transpose(rows, down_ref[...]))
        )
        pl.when(step == 6)(lambda: run(x_ref, heads_of))

    whole = lambda v: pl.BlockSpec(v.shape, lambda i, s: (0, 0))
    tokens = pl.BlockSpec((n, depth), lambda i, s: (2, 0)) if far else whole(x_all)
    return pl.pallas_call(
        kernel,
        out_shape=[jax.ShapeDtypeStruct((h, 6 * tile + 128), t) for t in types],
        grid_spec=pltpu.PrefetchScalarGridSpec(
            num_scalar_prefetch=1,
            grid=(7,),
            in_specs=[
                tokens,
                tokens,
                pl.BlockSpec((depth, tile), lambda i, s: (0, 2 * s[0] + jnp.minimum(i, 1))),
                pl.BlockSpec((depth, tile), lambda i, s: (0, 2 * s[0] + jnp.clip(i - 2, 0, 1))),
                pl.BlockSpec((tile, depth), lambda i, s: (2 * s[0] + jnp.clip(i - 4, 0, 1), 0)),
                whole(heads[0]),
                whole(heads[1]),
            ],
            out_specs=[pl.BlockSpec((h, tile), lambda i, s: (0, i)) for _ in types],
        ),
        compiler_params=params(),
        name="project_far" if far else "project_rest",
    )(core[None], x_all, u_all, *weights, *heads)


def joined(refs):
    return jnp.concatenate([ref[...] for ref in refs], 0)


def mixed(u_rows, slopes, head):
    slope = (
        slopes[:, 0:1].astype(F32) + slopes[:, 1:2].astype(F32) + slopes[:, 2:3].astype(F32)
    )
    return (u_rows.astype(F32) + slope * head).astype(BF)


def first_kernel(core, *refs):
    slopes, (turned_inputs, u_rows, head, gate, up, down_out, input_out, weight_out) = (
        refs[4:8],
        refs[8:],
    )
    step = pl.program_id(0)
    piece = joined(refs[:4])

    @pl.when(step == 0)
    def _():
        input_out[...] = jnp.zeros_like(input_out)

    @pl.when(step < 2)
    def _():
        down_out[...] = transpose_product(piece, mixed(u_rows[...], joined(slopes), head[...]))

    def run(weight):
        input_out[...] += right_transpose(piece, weight[...])
        weight_out[...] = product(turned_inputs[...], piece)

    pl.when((step >= 2) & (step < 4))(lambda: run(gate))
    pl.when(step >= 4)(lambda: run(up))


def first_products(core, pieces, gate_weight, up_weight, turned_inputs, u_rows, head):
    depth, count = turned_inputs.shape
    tile = gate_weight.shape[1] // 4
    h = count // 4
    whole = lambda v: pl.BlockSpec(v.shape, lambda i, s: (0, 0))
    return pl.pallas_call(
        first_kernel,
        out_shape=[
            jax.ShapeDtypeStruct((2 * tile, depth), F32),
            jax.ShapeDtypeStruct((count, depth), F32),
            jax.ShapeDtypeStruct((depth, 4 * tile), F32),
        ],
        grid_spec=pltpu.PrefetchScalarGridSpec(
            num_scalar_prefetch=1,
            grid=(6,),
            in_specs=[pl.BlockSpec((h, tile), lambda i, s: (0, i))] * 4
            + [pl.BlockSpec((h, 128), lambda i, s: (0, 6 * tile // 128))] * 4
            + [
                whole(turned_inputs),
                whole(u_rows),
                whole(head),
                pl.BlockSpec((depth, tile), lambda i, s: (0, 2 * s[0] + jnp.clip(i - 2, 0, 1))),
                pl.BlockSpec((depth, tile), lambda i, s: (0, 2 * s[0] + jnp.clip(i - 4, 0, 1))),
            ],
            out_specs=[
                pl.BlockSpec((tile, depth), lambda i, s: (jnp.minimum(i, 1), 0)),
                pl.BlockSpec((count, depth), lambda i, s: (0, 0)),
                pl.BlockSpec((depth, tile), lambda i, s: (0, jnp.maximum(i - 2, 0))),
            ],
        ),
        compiler_params=params(),
        name="first_products",
    )(core[None], *pieces, *pieces, turned_inputs, u_rows, head, gate_weight, up_weight)


def down_kernel(*refs):
    u_rows, head, near, out = refs[8:]
    out[...] = near[...] + transpose_product(
        joined(refs[:4]), mixed(u_rows[...], joined(refs[4:8]), head[...])
    )


def down_product(pieces, u_rows, head, near):
    width, depth = near.shape
    tile = width // 2
    h = pieces[0].shape[0]
    return pl.pallas_call(
        down_kernel,
        out_shape=jax.ShapeDtypeStruct((width, depth), F32),
        grid=(2,),
        in_specs=[pl.BlockSpec((h, tile), lambda i: (0, i))] * 4
        + [pl.BlockSpec((h, 128), lambda i: (0, 6 * tile // 128))] * 4
        + [
            pl.BlockSpec(u_rows.shape, lambda i: (0, 0)),
            pl.BlockSpec((1, depth), lambda i: (0, 0)),
            pl.BlockSpec((tile, depth), lambda i: (i, 0)),
        ],
        out_specs=pl.BlockSpec((tile, depth), lambda i: (i, 0)),
        compiler_params=params(),
        name="down_product",
    )(*pieces, *pieces, u_rows, head, near)


def input_kernel(core, source, *refs):
    gate, up, near, own_out, other_out, total = refs[4:]
    step = pl.program_id(0)
    piece = joined(refs[:4])
    n = near.shape[0]

    @pl.when(step == 0)
    def _():
        total[:n] = near[...]
        total[n:] = jnp.zeros((n, total.shape[1]), F32)

    def run(weight):
        total[n:] += right_transpose(piece, weight[...])

    pl.when(step < 2)(lambda: run(gate))
    pl.when(step >= 2)(lambda: run(up))

    @pl.when(step == pl.num_programs(0) - 1)
    def _():
        m = n // 8
        for i in range(8):
            own_out[i * m : (i + 1) * m] = total[pl.ds(pl.multiple_of(source[i] * m, m), m)]
            other_out[i * m : (i + 1) * m] = total[
                pl.ds(pl.multiple_of(source[8 + i] * m, m), m)
            ].astype(BF)


def input_product(core, source, pieces, gate_weight, up_weight, near):
    depth = gate_weight.shape[0]
    tile = gate_weight.shape[1] // 4
    h = pieces[0].shape[0]
    return pl.pallas_call(
        input_kernel,
        out_shape=[
            jax.ShapeDtypeStruct((4 * h, depth), F32),
            jax.ShapeDtypeStruct((4 * h, depth), BF),
        ],
        grid_spec=pltpu.PrefetchScalarGridSpec(
            num_scalar_prefetch=2,
            grid=(4,),
            in_specs=[pl.BlockSpec((h, tile), lambda i, s, t: (0, i + 2))] * 4
            + [
                pl.BlockSpec((depth, tile), lambda i, s, t: (0, 2 * s[0] + jnp.minimum(i, 1))),
                pl.BlockSpec(
                    (depth, tile), lambda i, s, t: (0, 2 * s[0] + jnp.maximum(i - 2, 0))
                ),
                pl.BlockSpec((4 * h, depth), lambda i, s, t: (0, 0)),
            ],
            out_specs=[pl.BlockSpec((4 * h, depth), lambda i, s, t: (0, 0))] * 2,
            scratch_shapes=[pltpu.VMEM((8 * h, depth), F32)],
        ),
        compiler_params=params(),
        name="input_product",
    )(core[None], source, *pieces, gate_weight, up_weight, near)


def weight_kernel(core, *refs):
    turned_inputs, near, keep_out, send_out = refs[4:]
    piece = joined(refs[:4])
    n = keep_out.shape[0]

    def product_of(first):
        rows = pl.ds(pl.multiple_of(first, n), n)
        return near[rows, :] + product(turned_inputs[rows, :], piece)

    keep_out[...] = product_of(core[0] * n)
    send_out[...] = product_of((1 - core[0]) * n).astype(BF)


def weight_product(core, pieces, turned_inputs, near):
    depth, width = near.shape
    tile = width // 4
    h = pieces[0].shape[0]
    return pl.pallas_call(
        weight_kernel,
        out_shape=[
            jax.ShapeDtypeStruct((depth // 2, width), F32),
            jax.ShapeDtypeStruct((depth // 2, width), BF),
        ],
        grid_spec=pltpu.PrefetchScalarGridSpec(
            num_scalar_prefetch=1,
            grid=(4,),
            in_specs=[pl.BlockSpec((h, tile), lambda i, s: (0, i + 2))] * 4
            + [
                pl.BlockSpec(turned_inputs.shape, lambda i, s: (0, 0)),
                pl.BlockSpec((depth, tile), lambda i, s: (0, i)),
            ],
            out_specs=[pl.BlockSpec((depth // 2, tile), lambda i, s: (0, i))] * 2,
        ),
        compiler_params=params(),
        name="weight_product",
    )(core[None], *pieces, turned_inputs, near)


def add_halves(direct, added, arrived, top_added):
    h, width = direct.shape
    if direct.dtype == F32:
        added = added + arrived.astype(F32)
        both = (added, direct) if top_added else (direct, added)
        return jnp.concatenate(both, 0).astype(BF)
    tile = (width - 128) // 6

    def kernel(direct_ref, added_ref, arrived_ref, out_ref):
        at = 0 if top_added else h
        out_ref[at : at + h] = (added_ref[...] + arrived_ref[...].astype(F32)).astype(BF)
        out_ref[h - at : 2 * h - at] = direct_ref[...].astype(BF)

    return pl.pallas_call(
        kernel,
        out_shape=jax.ShapeDtypeStruct((2 * h, width), BF),
        grid=(7,),
        in_specs=[pl.BlockSpec((h, tile), lambda i: (0, i))] * 3,
        out_specs=pl.BlockSpec((2 * h, tile), lambda i: (0, i)),
        compiler_params=params(16),
        name="add_halves",
    )(direct, added, arrived)


def ring_reduce(far, direct, added, own, ring):
    up, down = move(far[0], ring[1]), move(far[1], ring[3])
    up, down, *held = together(up, down, *direct, *added, *own)
    direct, added, own = held[:2], held[2:4], held[4:]
    below = move(add_halves(direct[0], added[0], up, True), ring[1])
    above = move(add_halves(direct[1], added[1], down, False), ring[3])
    h = own[0].shape[0]
    top = own[0] + below[:h].astype(F32) + above[:h].astype(F32)
    bottom = own[1] + below[h:].astype(F32) + above[h:].astype(F32)
    return top, bottom


def halves(value):
    h = value.shape[0] // 2
    return value[:h], value[h:]


def ring_start(top, bottom, ring):
    ahead_top, behind_bottom = move(top, ring[3]), move(bottom, ring[1])
    ahead_bottom, behind_top = move(bottom, ring[3]), move(top, ring[1])
    return ahead_top, ahead_bottom, behind_top, behind_bottom


def ring_pass(arrived, ring):
    return move(arrived[0], ring[3]), move(arrived[3], ring[1])


def per_device(
    inputs, gate_weight, up_weight, down_weight, reward_head, upstream, labels, label_mask
):
    tokens, depth = inputs.shape
    half = gate_weight.shape[1] // 2
    core = lax.axis_index("dp")
    row = lax.axis_index("row")
    z = lax.axis_index("col")
    y, x = row // SIDE, row % SIDE
    a = jnp.where(core == 0, x, y)
    b = jnp.where(core == 0, y, x)
    turn = (a + 4 - z) % 4
    mine = tokens // 2
    total = tokens * 8
    head_value = reward_head.astype(F32)
    weights = (gate_weight, up_weight)
    all_weights = (gate_weight, up_weight, down_weight)

    def around_z(value):
        return [value] + [move(value, AHEAD[4 - s]) for s in (1, 2, 3)]

    def both_cores(own, axis):
        other = move(own, OTHER)
        shape = own.shape[:axis] + (4, 1, tokens) + own.shape[axis + 1 :]
        own, other = own.reshape(shape), other.reshape(shape)
        return jnp.where(
            core == 0,
            jnp.concatenate([own, other], axis + 1),
            jnp.concatenate([other, own], axis + 1),
        )

    def ordered(whole):
        whole = lax.dynamic_slice_in_dim(jnp.concatenate([whole, whole], 0), turn, 4, 0)
        whole = lax.dynamic_slice_in_dim(jnp.concatenate([whole, whole], 1), b, 4, 1)
        return whole.reshape(total, depth)

    down_half = lax.dynamic_slice_in_dim(down_weight, core * half, half, 0)
    head_hidden = jnp.dot(down_half.astype(F32), head_value, precision=lax.Precision.HIGHEST)

    x_own, u_own = around_z(inputs), around_z(upstream)
    *x_own, head_hidden = together(*x_own, head_hidden)
    x_whole = both_cores(jnp.concatenate(x_own, 0), 0).reshape(4, 4, mine, depth)
    x_all = ordered(x_whole)
    u_all = ordered(both_cores(jnp.concatenate(u_own, 0), 0).reshape(4, 4, mine, depth))
    per_token = half // mine
    heads = (
        jnp.pad(reward_head[:, None], ((0, 0), (0, 127))),
        jnp.pad(head_hidden.reshape(mine, per_token), ((0, 0), (1, 127 - per_token))),
    )

    far = project(core, x_all, u_all, all_weights, heads, True)
    rest = project(core, x_all, u_all, all_weights, heads, False)
    top, bottom = ring_reduce(far, rest[:2], rest[2:4], rest[4:], FIRST)
    tags = both_cores(jnp.concatenate(around_z(jnp.stack([labels, label_mask])), 1), 1)
    late, later = tokens * 3, tokens * 7
    early_u = jnp.concatenate([u_all[later:], u_all[:late]], 0)
    early_x = jnp.concatenate([x_all[later:], x_all[:late]], 0).T
    late_u, late_x = u_all[late:later], x_all[late:later].T

    first, second = halves(top)
    third, fourth = halves(bottom)
    second, fourth = halves(second), halves(fourth)
    top, bottom = ring_reduce(
        halves(third.astype(BF)),
        (second[1], fourth[0]),
        (second[0], fourth[1]),
        halves(first),
        SECOND,
    )
    sums = jnp.concatenate([top, bottom], 0)

    gate, upper, grad_upstream = (sums[:, i * half : (i + 1) * half] for i in range(3))
    extra = sums[:, 3 * half :]
    own_inputs, head_hidden = extra[:, 0], extra[:, 1 : 1 + per_token].reshape(half)
    own_tags = lax.dynamic_slice_in_dim(
        tags.reshape(2, total), (turn * 4 + b) * mine, mine, 1
    ).astype(F32)
    sigmoid_gate = jax.nn.sigmoid(gate)
    hidden = (gate * sigmoid_gate * upper).astype(BF)

    part = jnp.sum(hidden.astype(F32) * head_hidden[None, :], axis=1)
    part = part + move(part, AHEAD[1]) + move(part, AHEAD[2]) + move(part, AHEAD[3])
    score = own_inputs + part + move(part, TWIN)
    slope = reward_weight * own_tags[1] * (jax.nn.sigmoid(score) - own_tags[0])
    grad_hidden = grad_upstream + slope[:, None] * head_hidden[None, :]
    grad_gate = (grad_hidden * upper * sigmoid_gate * (1.0 + gate * (1.0 - sigmoid_gate))).astype(
        BF
    )
    grad_upper = (grad_hidden * gate * sigmoid_gate).astype(BF)
    slopes = jnp.pad(jnp.stack(parts_of(slope, 3), axis=1), ((0, 0), (0, 125)))
    block = jnp.concatenate([hidden, grad_gate, grad_upper, slopes], axis=1)

    near = ring_start(*halves(block), SECOND)
    far = ring_pass(near, SECOND)
    top = jnp.concatenate([block, *near[:2]], 0)
    bottom = jnp.concatenate([*far, *near[2:]], 0)
    near = ring_start(top, bottom, FIRST)
    far = ring_pass(near, FIRST)
    head_row = head_value[None, :]
    early = (near[3], top, bottom, near[0])
    near_down, near_input, near_weight = first_products(
        core, early, *weights, early_x, early_u, head_row
    )
    *last, near_down, near_input, near_weight = together(
        near[1], *far, near[2], near_down, near_input, near_weight
    )

    spot = jnp.arange(16, dtype=jnp.int32)
    whose = jnp.where(spot < 8, core, 1 - core)
    ahead_of = (z + (spot // 2) % 4 + 4 - a) % 4
    source = ahead_of * 4 + (whose * 2 + spot % 2 + 4 - b) % 4
    source_early = (source + 2) % 16
    own_part, other_part = input_product(core, source_early, last, *weights, near_input)
    near_weight, own_part = together(near_weight, own_part)
    other_arrived = move(other_part, OTHER)
    keep, send = weight_product(core, last, late_x, near_weight)
    other = move(send, OTHER)
    near_down, other_arrived = together(near_down, other_arrived)
    blocks = jnp.split(own_part + other_arrived.astype(F32), 4, 0)
    input_sum = blocks[0]
    blocks = [t.astype(BF) for t in blocks[1:]]
    *blocks, near_down = together(*blocks, near_down)
    arrived = [move(blocks[s - 1], AHEAD[s]) for s in (1, 2, 3)]
    down_grad = down_product(last, late_u, head_row, near_down)

    slope_parts = jnp.concatenate(
        [
            p[:, 6 * (half // 2) :]
            for p in (top, bottom, near[0], *last, near[3])
        ],
        0,
    )
    slope_all = slope_parts[:, :3].astype(F32).sum(1)
    own_slope = jnp.concatenate(
        [lax.dynamic_slice_in_dim(slope_all, source[i] * mine, mine, 0) for i in range(2)]
    )

    def both_halves(start):
        k, o = keep[:, start : start + half], other[:, start : start + half].astype(F32)
        return jnp.concatenate([jnp.where(core == 0, k, o), jnp.where(core == 0, o, k)], axis=1)

    gate_grad, up_grad = both_halves(0), both_halves(half)
    *arrived, gate_grad, up_grad, down_grad = together(*arrived, gate_grad, up_grad, down_grad)
    for t in arrived:
        input_sum = input_sum + t.astype(F32)
    input_grad = upstream.astype(F32) + own_slope[:, None] * head_value[None, :] + input_sum
    return (gate_grad, up_grad, down_grad, input_grad)


def solution(mesh):
    in_specs = (
        P(("col", "dp"), "row"),
        P("row", "col"),
        P("row", "col"),
        P("col", "row"),
        P("row"),
        P(("col", "dp"), "row"),
        P(("col", "dp")),
        P(("col", "dp")),
    )
    out_specs = (
        P(("row", "dp"), "col"),
        P(("row", "dp"), "col"),
        P(("col", "dp"), "row"),
        P(("col", "dp"), "row"),
    )
    return jax.shard_map(
        per_device, mesh=mesh, in_specs=in_specs, out_specs=out_specs, check_vma=False
    )
```

```python
import jax
import jax.numpy as jnp
from jax import lax
from jax.experimental import pallas as pl
from jax.experimental.pallas import tpu as pltpu
from jax.sharding import PartitionSpec as P

reward_weight = 8.0
BF = jnp.bfloat16
F32 = jnp.float32
AXES = ("row", "col", "dp")
SIDE = 4


def transpose_product(left, right):
    return lax.dot_general(
        left, right, (((0,), (0,)), ((), ())), preferred_element_type=F32
    )


def right_transpose(left, right):
    return lax.dot_general(
        left, right, (((1,), (1,)), ((), ())), preferred_element_type=F32
    )


def product(left, right):
    return jnp.dot(left, right, preferred_element_type=F32)


def flat(y, x, z, c):
    return ((y * SIDE + x) * 4 + z) * 2 + c


def pairs(move):
    found = []
    for y in range(SIDE):
        for x in range(SIDE):
            for z in range(4):
                for c in range(2):
                    found.append((flat(y, x, z, c), flat(*move(y, x, z, c))))
    return found


def step_first(s):
    return pairs(
        lambda y, x, z, c: (y, (x + s) % SIDE, z, c) if c == 0 else ((y + s) % SIDE, x, z, c)
    )


def step_second(s):
    return pairs(
        lambda y, x, z, c: ((y + s) % SIDE, x, z, c) if c == 0 else (y, (x + s) % SIDE, z, c)
    )


FIRST = {s: step_first(s) for s in (1, 2, 3)}
SECOND = {s: step_second(s) for s in (1, 2, 3)}


def move(value, links):
    return lax.ppermute(value, AXES, links)


AHEAD = {s: pairs(lambda y, x, z, c, s=s: (y, x, (z + s) % 4, c)) for s in (1, 2, 3)}
OTHER = pairs(lambda y, x, z, c: (y, x, z, 1 - c))


def together(*values):
    return lax.optimization_barrier(values)


def parts_of(value, n):
    found = []
    for _ in range(n):
        found.append(value.astype(BF))
        value = value - found[-1].astype(F32)
    return found


def params(mib=24):
    return pltpu.CompilerParams(vmem_limit_bytes=mib << 20)


def project(core, x_all, u_all, weights, heads, far):
    total, depth = x_all.shape
    tile = weights[0].shape[1] // 4
    n = total // 4
    h = n // 2
    spread = heads[1].shape[0]
    starts = (0, h) if far else (n + h, 3 * n, n, 3 * n + h, 0, h)
    types = (BF, BF) if far else (BF, BF, F32, F32, F32, F32)

    def kernel(core_ref, x_ref, u_ref, gate_ref, up_ref, down_ref, head_ref, spread_ref, *outs):
        step = pl.program_id(0)

        def run(rows_ref, of):
            for start, out in zip(starts, outs):
                value = of(rows_ref[start : start + h])
                out[:, : value.shape[1]] = value.astype(out.dtype)

        def heads_of(rows):
            return product(rows, head_ref[...]) + jnp.concatenate(
                [spread_ref[...]] * (h // spread), 0
            )

        pl.when(step < 2)(lambda: run(x_ref, lambda rows: product(rows, gate_ref[...])))
        pl.when((step >= 2) & (step < 4))(
            lambda: run(x_ref, lambda rows: product(rows, up_ref[...]))
        )
        pl.when((step >= 4) & (step < 6))(
            lambda: run(u_ref, lambda rows: right_transpose(rows, down_ref[...]))
        )
        pl.when(step == 6)(lambda: run(x_ref, heads_of))

    whole = lambda v: pl.BlockSpec(v.shape, lambda i, s: (0, 0))
    tokens = pl.BlockSpec((n, depth), lambda i, s: (2, 0)) if far else whole(x_all)
    return pl.pallas_call(
        kernel,
        out_shape=[jax.ShapeDtypeStruct((h, 6 * tile + 128), t) for t in types],
        grid_spec=pltpu.PrefetchScalarGridSpec(
            num_scalar_prefetch=1,
            grid=(7,),
            in_specs=[
                tokens,
                tokens,
                pl.BlockSpec((depth, tile), lambda i, s: (0, 2 * s[0] + jnp.minimum(i, 1))),
                pl.BlockSpec((depth, tile), lambda i, s: (0, 2 * s[0] + jnp.clip(i - 2, 0, 1))),
                pl.BlockSpec((tile, depth), lambda i, s: (2 * s[0] + jnp.clip(i - 4, 0, 1), 0)),
                whole(heads[0]),
                whole(heads[1]),
            ],
            out_specs=[pl.BlockSpec((h, tile), lambda i, s: (0, i)) for _ in types],
        ),
        compiler_params=params(),
        name="project_far" if far else "project_rest",
    )(core[None], x_all, u_all, *weights, *heads)


def joined(refs):
    return jnp.concatenate([ref[...] for ref in refs], 0)


def pairs_of(refs):
    return [
        jnp.concatenate([refs[i][...], refs[i + 1][...]], 0) for i in range(0, len(refs), 2)
    ]


def mixed(u_rows, slopes, head):
    slope = (
        slopes[:, 0:1].astype(F32) + slopes[:, 1:2].astype(F32) + slopes[:, 2:3].astype(F32)
    )
    return (u_rows.astype(F32) + slope * head).astype(BF)


def near_kernel(*refs):
    pieces, slopes, refs = pairs_of(refs[:6]), refs[6:12], refs[12:]
    turned_inputs, u_all, head, weight, down_out, input_out, weight_out = refs
    step = pl.program_id(0)
    n = pieces[0].shape[0]
    starts = (0, n, 3 * n)

    @pl.when(step == 0)
    def _():
        input_out[...] = jnp.zeros_like(input_out)

    @pl.when(step < 2)
    def _():
        found = None
        for piece, slope, at in zip(pieces, pairs_of(slopes), starts):
            term = transpose_product(piece, mixed(u_all[at : at + n], slope, head[...]))
            found = term if found is None else found + term
        down_out[...] = found

    @pl.when(step >= 2)
    def _():
        found = None
        for i, piece in enumerate(pieces):
            input_out[i * n : (i + 1) * n] += product(piece, weight[...])
            term = product(turned_inputs[:, starts[i] : starts[i] + n], piece)
            found = term if found is None else found + term
        weight_out[...] = found


def near_products(pieces, turned_weight, turned_inputs, u_all, head):
    depth, total = turned_inputs.shape
    tile = turned_weight.shape[0] // 4
    h = pieces[0].shape[0]
    n = 2 * h
    return pl.pallas_call(
        near_kernel,
        out_shape=[
            jax.ShapeDtypeStruct((2 * tile, depth), F32),
            jax.ShapeDtypeStruct((3 * n, depth), F32),
            jax.ShapeDtypeStruct((depth, 4 * tile), F32),
        ],
        grid_spec=pl.GridSpec(
            grid=(6,),
            in_specs=[pl.BlockSpec((h, tile), lambda i: (0, i))] * 6
            + [pl.BlockSpec((h, 128), lambda i: (0, 6 * tile // 128))] * 6
            + [
                pl.BlockSpec((depth, total), lambda i: (0, 0)),
                pl.BlockSpec((total, depth), lambda i: (0, 0)),
                pl.BlockSpec((1, depth), lambda i: (0, 0)),
                pl.BlockSpec((tile, depth), lambda i: (jnp.maximum(i - 2, 0), 0)),
            ],
            out_specs=[
                pl.BlockSpec((tile, depth), lambda i: (jnp.minimum(i, 1), 0)),
                pl.BlockSpec((3 * n, depth), lambda i: (0, 0)),
                pl.BlockSpec((depth, tile), lambda i: (0, jnp.maximum(i - 2, 0))),
            ],
        ),
        compiler_params=params(24),
        name="near_products",
    )(*pieces, *pieces, turned_inputs, u_all, head, turned_weight)


def down_kernel(top, bottom, slope_top, slope_bottom, u_far, head, near, out):
    slopes = jnp.concatenate([slope_top[...], slope_bottom[...]], 0)
    rows = jnp.concatenate([top[...], bottom[...]], 0)
    out[...] = near[...] + transpose_product(rows, mixed(u_far[...], slopes, head[...]))


def down_product(top, bottom, u_all, head, near):
    width, depth = near.shape
    tile = width // 2
    h = top.shape[0]
    piece = pl.BlockSpec((h, tile), lambda i: (0, i))
    slope = pl.BlockSpec((h, 128), lambda i: (0, 6 * tile // 128))
    return pl.pallas_call(
        down_kernel,
        out_shape=jax.ShapeDtypeStruct((width, depth), F32),
        grid=(2,),
        in_specs=[
            piece,
            piece,
            slope,
            slope,
            pl.BlockSpec((2 * h, depth), lambda i: (2, 0)),
            pl.BlockSpec((1, depth), lambda i: (0, 0)),
            pl.BlockSpec((tile, depth), lambda i: (i, 0)),
        ],
        out_specs=pl.BlockSpec((tile, depth), lambda i: (i, 0)),
        compiler_params=params(24),
        name="down_product",
    )(top, bottom, top, bottom, u_all, head, near)


def turn_kernel(core, gate, up, out):
    del core
    step = pl.program_id(0)

    @pl.when(step < 2)
    def _():
        out[...] = gate[...].T

    @pl.when(step >= 2)
    def _():
        out[...] = up[...].T


def turned_columns(core, gate_weight, up_weight):
    depth, width = gate_weight.shape
    tile = width // 4
    return pl.pallas_call(
        turn_kernel,
        out_shape=jax.ShapeDtypeStruct((width, depth), BF),
        grid_spec=pltpu.PrefetchScalarGridSpec(
            num_scalar_prefetch=1,
            grid=(4,),
            in_specs=[
                pl.BlockSpec((depth, tile), lambda i, s: (0, 2 * s[0] + jnp.minimum(i, 1))),
                pl.BlockSpec((depth, tile), lambda i, s: (0, 2 * s[0] + jnp.maximum(i - 2, 0))),
            ],
            out_specs=pl.BlockSpec((tile, depth), lambda i, s: (i, 0)),
        ),
        compiler_params=params(16),
        name="turned_columns",
    )(core[None], gate_weight, up_weight)


def input_kernel(source, top, bottom, weight, near, own_out, other_out, total):
    step = pl.program_id(0)
    n = near.shape[0] // 3
    h = n // 2

    @pl.when(step == 0)
    def _():
        total[: 2 * n] = near[: 2 * n]
        total[2 * n : 3 * n] = jnp.zeros((n, total.shape[1]), F32)
        total[3 * n :] = near[2 * n :]

    total[2 * n : 2 * n + h] += product(top[...], weight[...])
    total[2 * n + h : 3 * n] += product(bottom[...], weight[...])

    @pl.when(step == pl.num_programs(0) - 1)
    def _():
        m = n // 4
        for i in range(8):
            own_out[i * m : (i + 1) * m] = total[pl.ds(pl.multiple_of(source[i] * m, m), m)]
            other_out[i * m : (i + 1) * m] = total[
                pl.ds(pl.multiple_of(source[8 + i] * m, m), m)
            ].astype(BF)


def input_product(source, top, bottom, turned_weight, near):
    depth = turned_weight.shape[1]
    tile = turned_weight.shape[0] // 4
    h = top.shape[0]
    return pl.pallas_call(
        input_kernel,
        out_shape=[
            jax.ShapeDtypeStruct((4 * h, depth), F32),
            jax.ShapeDtypeStruct((4 * h, depth), BF),
        ],
        grid_spec=pltpu.PrefetchScalarGridSpec(
            num_scalar_prefetch=1,
            grid=(4,),
            in_specs=[pl.BlockSpec((h, tile), lambda i, s: (0, i + 2))] * 2
            + [
                pl.BlockSpec((tile, depth), lambda i, s: (i, 0)),
                pl.BlockSpec((6 * h, depth), lambda i, s: (0, 0)),
            ],
            out_specs=[pl.BlockSpec((4 * h, depth), lambda i, s: (0, 0))] * 2,
            scratch_shapes=[pltpu.VMEM((8 * h, depth), F32)],
        ),
        compiler_params=params(24),
        name="input_product",
    )(source, top, bottom, turned_weight, near)


def weight_kernel(core, top, bottom, turned_inputs, near, gate_out, up_out, send_out):
    step = pl.program_id(0)
    n = gate_out.shape[0]
    h = top.shape[0]
    piece = joined((top, bottom))

    def product_of(first):
        rows = pl.ds(pl.multiple_of(first, n), n)
        return near[rows, :] + product(turned_inputs[rows, 4 * h : 6 * h], piece)

    def keep(out):
        out[...] = product_of(core[0] * n)

    pl.when(step < 2)(lambda: keep(gate_out))
    pl.when(step >= 2)(lambda: keep(up_out))
    send_out[...] = product_of((1 - core[0]) * n).astype(BF)


def weight_product(core, top, bottom, turned_inputs, near):
    depth, width = near.shape
    tile = width // 4
    h = top.shape[0]
    rows = depth // 2
    return pl.pallas_call(
        weight_kernel,
        out_shape=[
            jax.ShapeDtypeStruct((rows, width), F32),
            jax.ShapeDtypeStruct((rows, width), F32),
            jax.ShapeDtypeStruct((rows, width), BF),
        ],
        grid_spec=pltpu.PrefetchScalarGridSpec(
            num_scalar_prefetch=1,
            grid=(4,),
            in_specs=[pl.BlockSpec((h, tile), lambda i, s: (0, i + 2))] * 2
            + [
                pl.BlockSpec(turned_inputs.shape, lambda i, s: (0, 0)),
                pl.BlockSpec((depth, tile), lambda i, s: (0, i)),
            ],
            out_specs=[
                pl.BlockSpec((rows, tile), lambda i, s: (0, 2 * s[0] + jnp.minimum(i, 1))),
                pl.BlockSpec((rows, tile), lambda i, s: (0, 2 * s[0] + jnp.maximum(i - 2, 0))),
                pl.BlockSpec((rows, tile), lambda i, s: (0, i)),
            ],
        ),
        compiler_params=params(24),
        name="weight_product",
    )(core[None], top, bottom, turned_inputs, near)


def fill_kernel(core, gate_part, up_part, gate_in, up_in, gate_out, up_out):
    del core, gate_in, up_in
    gate_out[...] = gate_part[...].astype(F32)
    up_out[...] = up_part[...].astype(F32)


def fill_columns(core, other, gate_grad, up_grad):
    rows, width = gate_grad.shape
    tile = width // 4
    part = lambda first: pl.BlockSpec((rows, tile), lambda i, s: (0, first + i))
    target = pl.BlockSpec((rows, tile), lambda i, s: (0, 2 - 2 * s[0] + i))
    return pl.pallas_call(
        fill_kernel,
        out_shape=[jax.ShapeDtypeStruct((rows, width), F32)] * 2,
        grid_spec=pltpu.PrefetchScalarGridSpec(
            num_scalar_prefetch=1,
            grid=(2,),
            in_specs=[part(0), part(2)] + [pl.BlockSpec(memory_space=pl.ANY)] * 2,
            out_specs=[target] * 2,
        ),
        input_output_aliases={3: 0, 4: 1},
        compiler_params=params(16),
        name="fill_columns",
    )(core[None], other, other, gate_grad, up_grad)


def add_halves(direct, added, arrived, top_added):
    h, width = direct.shape
    if direct.dtype == F32:
        added = added + arrived.astype(F32)
        both = (added, direct) if top_added else (direct, added)
        return jnp.concatenate(both, 0).astype(BF)
    tile = (width - 128) // 6

    def kernel(direct_ref, added_ref, arrived_ref, out_ref):
        at = 0 if top_added else h
        out_ref[at : at + h] = (added_ref[...] + arrived_ref[...].astype(F32)).astype(BF)
        out_ref[h - at : 2 * h - at] = direct_ref[...].astype(BF)

    return pl.pallas_call(
        kernel,
        out_shape=jax.ShapeDtypeStruct((2 * h, width), BF),
        grid=(7,),
        in_specs=[pl.BlockSpec((h, tile), lambda i: (0, i))] * 3,
        out_specs=pl.BlockSpec((2 * h, tile), lambda i: (0, i)),
        compiler_params=params(16),
        name="add_halves",
    )(direct, added, arrived)


def ring_reduce(far, direct, added, own, ring):
    up, down = move(far[0], ring[1]), move(far[1], ring[3])
    up, down, *held = together(up, down, *direct, *added, *own)
    direct, added, own = held[:2], held[2:4], held[4:]
    below = move(add_halves(direct[0], added[0], up, True), ring[1])
    above = move(add_halves(direct[1], added[1], down, False), ring[3])
    h = own[0].shape[0]
    top = own[0] + below[:h].astype(F32) + above[:h].astype(F32)
    bottom = own[1] + below[h:].astype(F32) + above[h:].astype(F32)
    return top, bottom


def halves(value):
    h = value.shape[0] // 2
    return value[:h], value[h:]


def ring_start(top, bottom, ring):
    ahead_top, behind_bottom = move(top, ring[3]), move(bottom, ring[1])
    ahead_bottom, behind_top = move(bottom, ring[3]), move(top, ring[1])
    return ahead_top, ahead_bottom, behind_top, behind_bottom


def ring_pass(arrived, ring):
    return move(arrived[0], ring[3]), move(arrived[3], ring[1])


def per_device(
    inputs, gate_weight, up_weight, down_weight, reward_head, upstream, labels, label_mask
):
    tokens, depth = inputs.shape
    half = gate_weight.shape[1] // 2
    core = lax.axis_index("dp")
    row = lax.axis_index("row")
    z = lax.axis_index("col")
    y, x = row // SIDE, row % SIDE
    turn = (x + 4 - z) % 4
    mine = tokens // 2
    total = tokens * 8
    head_value = reward_head.astype(F32)
    all_weights = (gate_weight, up_weight, down_weight)

    def around_z(value):
        return [value] + [move(value, AHEAD[4 - s]) for s in (1, 2, 3)]

    def both_cores(own, axis):
        other = move(own, OTHER)
        shape = own.shape[:axis] + (4, 1, tokens) + own.shape[axis + 1 :]
        own, other = own.reshape(shape), other.reshape(shape)
        return jnp.where(
            core == 0,
            jnp.concatenate([own, other], axis + 1),
            jnp.concatenate([other, own], axis + 1),
        )

    def ordered(whole):
        whole = lax.dynamic_slice_in_dim(jnp.concatenate([whole, whole], 0), turn, 4, 0)
        whole = lax.dynamic_slice_in_dim(jnp.concatenate([whole, whole], 1), y, 4, 1)
        return jnp.where(core == 0, whole, whole.transpose(1, 0, 2, 3)).reshape(total, depth)

    down_half = lax.dynamic_slice_in_dim(down_weight, core * half, half, 0)
    head_hidden = jnp.dot(down_half.astype(F32), head_value, precision=lax.Precision.HIGHEST)

    x_own, u_own = around_z(inputs), around_z(upstream)
    *x_own, head_hidden = together(*x_own, head_hidden)
    x_whole = both_cores(jnp.concatenate(x_own, 0), 0).reshape(4, 4, mine, depth)
    x_all = ordered(x_whole)
    u_all = ordered(both_cores(jnp.concatenate(u_own, 0), 0).reshape(4, 4, mine, depth))
    per_token = half // mine
    heads = (
        jnp.pad(reward_head[:, None], ((0, 0), (0, 127))),
        jnp.pad(head_hidden.reshape(mine, per_token), ((0, 0), (1, 127 - per_token))),
    )

    far = project(core, x_all, u_all, all_weights, heads, True)
    rest = project(core, x_all, u_all, all_weights, heads, False)
    top, bottom = ring_reduce(far, rest[:2], rest[2:4], rest[4:], FIRST)
    tags = both_cores(jnp.concatenate(around_z(jnp.stack([labels, label_mask])), 1), 1)
    turned_inputs = x_all.T
    turned_weight = turned_columns(core, gate_weight, up_weight)

    first, second = halves(top)
    third, fourth = halves(bottom)
    second, fourth = halves(second), halves(fourth)
    top, bottom = ring_reduce(
        halves(third.astype(BF)),
        (second[1], fourth[0]),
        (second[0], fourth[1]),
        halves(first),
        SECOND,
    )
    sums = jnp.concatenate([top, bottom], 0)

    gate, upper, grad_upstream = (sums[:, i * half : (i + 1) * half] for i in range(3))
    extra = sums[:, 3 * half :]
    own_inputs, head_hidden = extra[:, 0], extra[:, 1 : 1 + per_token].reshape(half)
    own_tags = lax.dynamic_slice_in_dim(
        tags.reshape(2, total), (turn * 4 + y) * mine, mine, 1
    ).astype(F32)
    sigmoid_gate = jax.nn.sigmoid(gate)
    hidden = (gate * sigmoid_gate * upper).astype(BF)

    part = jnp.sum(hidden.astype(F32) * head_hidden[None, :], axis=1)
    part = part + move(part, AHEAD[1]) + move(part, AHEAD[2]) + move(part, AHEAD[3])
    score = own_inputs + part + move(part, OTHER)
    slope = reward_weight * own_tags[1] * (jax.nn.sigmoid(score) - own_tags[0])
    grad_hidden = grad_upstream + slope[:, None] * head_hidden[None, :]
    grad_gate = (grad_hidden * upper * sigmoid_gate * (1.0 + gate * (1.0 - sigmoid_gate))).astype(
        BF
    )
    grad_upper = (grad_hidden * gate * sigmoid_gate).astype(BF)
    slopes = jnp.pad(jnp.stack(parts_of(slope, 3), axis=1), ((0, 0), (0, 125)))
    block = jnp.concatenate([hidden, grad_gate, grad_upper, slopes], axis=1)

    near = ring_start(*halves(block), SECOND)
    far = ring_pass(near, SECOND)
    top = jnp.concatenate([block, *near[:2]], 0)
    bottom = jnp.concatenate([*far, *near[2:]], 0)
    near = ring_start(top, bottom, FIRST)
    far_top, far_bottom = ring_pass(near, FIRST)

    head_row = head_value[None, :]
    near_down, near_input, near_weight = near_products(
        [top, bottom, *near], turned_weight, turned_inputs, u_all, head_row
    )
    far_top, far_bottom, near_down, near_weight, near_input = together(
        far_top, far_bottom, near_down, near_weight, near_input
    )

    spot = jnp.arange(16, dtype=jnp.int32)
    whose = jnp.where(spot < 8, core, 1 - core)
    along_x = (z + (spot // 2) % 4 + 4 - x) % 4
    along_y = (whose * 2 + spot % 2 + 4 - y) % 4
    source = jnp.where(core == 0, along_x * 4 + along_y, along_y * 4 + along_x)
    last = (far_top, far_bottom)
    own_part, other_part = input_product(source, *last, turned_weight, near_input)
    near_weight, own_part = together(near_weight, own_part)
    other_arrived = move(other_part, OTHER)
    gate_grad, up_grad, send = weight_product(core, *last, turned_inputs, near_weight)
    other = move(send, OTHER)
    near_down, other_arrived = together(near_down, other_arrived)
    blocks = jnp.split(own_part + other_arrived.astype(F32), 4, 0)
    input_sum = blocks[0]
    blocks = [t.astype(BF) for t in blocks[1:]]
    *blocks, near_down = together(*blocks, near_down)
    arrived = [move(blocks[s - 1], AHEAD[s]) for s in (1, 2, 3)]
    down_grad = down_product(*last, u_all, head_row, near_down)

    slope_parts = jnp.concatenate(
        [
            p[:, 6 * (half // 2) :]
            for p in (top, bottom, *near[:2], far_top, far_bottom, *near[2:])
        ],
        0,
    )
    slope_all = slope_parts[:, :3].astype(F32).sum(1)
    own_slope = jnp.concatenate(
        [lax.dynamic_slice_in_dim(slope_all, source[i] * mine, mine, 0) for i in range(2)]
    )

    gate_grad, up_grad = fill_columns(core, other, gate_grad, up_grad)
    *arrived, gate_grad, up_grad, down_grad = together(*arrived, gate_grad, up_grad, down_grad)
    for t in arrived:
        input_sum = input_sum + t.astype(F32)
    input_grad = upstream.astype(F32) + own_slope[:, None] * head_value[None, :] + input_sum
    return (gate_grad, up_grad, down_grad, input_grad)


def solution(mesh):
    in_specs = (
        P(("col", "dp"), "row"),
        P("row", "col"),
        P("row", "col"),
        P("col", "row"),
        P("row"),
        P(("col", "dp"), "row"),
        P(("col", "dp")),
        P(("col", "dp")),
    )
    out_specs = (
        P(("row", "dp"), "col"),
        P(("row", "dp"), "col"),
        P(("col", "dp"), "row"),
        P(("col", "dp"), "row"),
    )
    return jax.shard_map(
        per_device, mesh=mesh, in_specs=in_specs, out_specs=out_specs, check_vma=False
    )
```

```python
import jax
import jax.numpy as jnp
from jax import lax
from jax.experimental import pallas as pl
from jax.experimental.pallas import tpu as pltpu
from jax.sharding import PartitionSpec as P

reward_weight = 8.0
BF = jnp.bfloat16
F32 = jnp.float32
AXES = ("row", "col", "dp")
SIDE = 4


def transpose_product(left, right):
    return lax.dot_general(
        left, right, (((0,), (0,)), ((), ())), preferred_element_type=F32
    )


def right_transpose(left, right):
    return lax.dot_general(
        left, right, (((1,), (1,)), ((), ())), preferred_element_type=F32
    )


def product(left, right):
    return jnp.dot(left, right, preferred_element_type=F32)


def flat(y, x, z, c):
    return ((y * SIDE + x) * 4 + z) * 2 + c


def pairs(move):
    found = []
    for y in range(SIDE):
        for x in range(SIDE):
            for z in range(4):
                for c in range(2):
                    found.append((flat(y, x, z, c), flat(*move(y, x, z, c))))
    return found


def step_first(s):
    return pairs(
        lambda y, x, z, c: (y, (x + s) % SIDE, z, c) if c == 0 else ((y + s) % SIDE, x, z, c)
    )


def step_second(s):
    return pairs(
        lambda y, x, z, c: ((y + s) % SIDE, x, z, c) if c == 0 else (y, (x + s) % SIDE, z, c)
    )


FIRST = {s: step_first(s) for s in (1, 2, 3)}
SECOND = {s: step_second(s) for s in (1, 2, 3)}


def move(value, links):
    return lax.ppermute(value, AXES, links)


AHEAD = {s: pairs(lambda y, x, z, c, s=s: (y, x, (z + s) % 4, c)) for s in (1, 2, 3)}
OTHER = pairs(lambda y, x, z, c: (y, x, z, 1 - c))


def together(*values):
    return lax.optimization_barrier(values)


def parts_of(value, n):
    found = []
    for _ in range(n):
        found.append(value.astype(BF))
        value = value - found[-1].astype(F32)
    return found


def params(mib=24):
    return pltpu.CompilerParams(vmem_limit_bytes=mib << 20)


def project(core, x_all, u_all, weights, heads, far):
    total, depth = x_all.shape
    tile = weights[0].shape[1] // 4
    n = total // 4
    h = n // 2
    spread = heads[1].shape[0]
    starts = (0, h) if far else (n + h, 3 * n, n, 3 * n + h, 0, h)
    types = (BF, BF) if far else (BF, BF, F32, F32, F32, F32)

    def kernel(core_ref, x_ref, u_ref, gate_ref, up_ref, down_ref, head_ref, spread_ref, *outs):
        step = pl.program_id(0)

        def run(rows_ref, of):
            for start, out in zip(starts, outs):
                value = of(rows_ref[start : start + h])
                out[:, : value.shape[1]] = value.astype(out.dtype)

        def heads_of(rows):
            return product(rows, head_ref[...]) + jnp.concatenate(
                [spread_ref[...]] * (h // spread), 0
            )

        pl.when(step < 2)(lambda: run(x_ref, lambda rows: product(rows, gate_ref[...])))
        pl.when((step >= 2) & (step < 4))(
            lambda: run(x_ref, lambda rows: product(rows, up_ref[...]))
        )
        pl.when((step >= 4) & (step < 6))(
            lambda: run(u_ref, lambda rows: right_transpose(rows, down_ref[...]))
        )
        pl.when(step == 6)(lambda: run(x_ref, heads_of))

    whole = lambda v: pl.BlockSpec(v.shape, lambda i, s: (0, 0))
    tokens = pl.BlockSpec((n, depth), lambda i, s: (2, 0)) if far else whole(x_all)
    return pl.pallas_call(
        kernel,
        out_shape=[jax.ShapeDtypeStruct((h, 6 * tile + 128), t) for t in types],
        grid_spec=pltpu.PrefetchScalarGridSpec(
            num_scalar_prefetch=1,
            grid=(7,),
            in_specs=[
                tokens,
                tokens,
                pl.BlockSpec((depth, tile), lambda i, s: (0, 2 * s[0] + jnp.minimum(i, 1))),
                pl.BlockSpec((depth, tile), lambda i, s: (0, 2 * s[0] + jnp.clip(i - 2, 0, 1))),
                pl.BlockSpec((tile, depth), lambda i, s: (2 * s[0] + jnp.clip(i - 4, 0, 1), 0)),
                whole(heads[0]),
                whole(heads[1]),
            ],
            out_specs=[pl.BlockSpec((h, tile), lambda i, s: (0, i)) for _ in types],
        ),
        compiler_params=params(),
        name="project_far" if far else "project_rest",
    )(core[None], x_all, u_all, *weights, *heads)


def joined(refs):
    return jnp.concatenate([ref[...] for ref in refs], 0)


def pairs_of(refs):
    return [
        jnp.concatenate([refs[i][...], refs[i + 1][...]], 0) for i in range(0, len(refs), 2)
    ]


def mixed(u_rows, slopes, head):
    slope = (
        slopes[:, 0:1].astype(F32) + slopes[:, 1:2].astype(F32) + slopes[:, 2:3].astype(F32)
    )
    return (u_rows.astype(F32) + slope * head).astype(BF)


def near_kernel(*refs):
    pieces, slopes, refs = pairs_of(refs[:6]), refs[6:12], refs[12:]
    turned_inputs, u_all, head, weight, down_out, input_out, weight_out = refs
    step = pl.program_id(0)
    n = pieces[0].shape[0]
    starts = (0, n, 3 * n)

    @pl.when(step == 0)
    def _():
        input_out[...] = jnp.zeros_like(input_out)

    @pl.when(step < 2)
    def _():
        found = None
        for piece, slope, at in zip(pieces, pairs_of(slopes), starts):
            term = transpose_product(piece, mixed(u_all[at : at + n], slope, head[...]))
            found = term if found is None else found + term
        down_out[...] = found

    @pl.when(step >= 2)
    def _():
        found = None
        for i, piece in enumerate(pieces):
            input_out[i * n : (i + 1) * n] += product(piece, weight[...])
            term = product(turned_inputs[:, starts[i] : starts[i] + n], piece)
            found = term if found is None else found + term
        weight_out[...] = found


def near_products(pieces, turned_weight, turned_inputs, u_all, head):
    depth, total = turned_inputs.shape
    tile = turned_weight.shape[0] // 4
    h = pieces[0].shape[0]
    n = 2 * h
    return pl.pallas_call(
        near_kernel,
        out_shape=[
            jax.ShapeDtypeStruct((2 * tile, depth), F32),
            jax.ShapeDtypeStruct((3 * n, depth), F32),
            jax.ShapeDtypeStruct((depth, 4 * tile), F32),
        ],
        grid_spec=pl.GridSpec(
            grid=(6,),
            in_specs=[pl.BlockSpec((h, tile), lambda i: (0, i))] * 6
            + [pl.BlockSpec((h, 128), lambda i: (0, 6 * tile // 128))] * 6
            + [
                pl.BlockSpec((depth, total), lambda i: (0, 0)),
                pl.BlockSpec((total, depth), lambda i: (0, 0)),
                pl.BlockSpec((1, depth), lambda i: (0, 0)),
                pl.BlockSpec((tile, depth), lambda i: (jnp.maximum(i - 2, 0), 0)),
            ],
            out_specs=[
                pl.BlockSpec((tile, depth), lambda i: (jnp.minimum(i, 1), 0)),
                pl.BlockSpec((3 * n, depth), lambda i: (0, 0)),
                pl.BlockSpec((depth, tile), lambda i: (0, jnp.maximum(i - 2, 0))),
            ],
        ),
        compiler_params=params(54),
        name="near_products",
    )(*pieces, *pieces, turned_inputs, u_all, head, turned_weight)


def down_kernel(top, bottom, slope_top, slope_bottom, u_far, head, near, out):
    slopes = jnp.concatenate([slope_top[...], slope_bottom[...]], 0)
    rows = jnp.concatenate([top[...], bottom[...]], 0)
    out[...] = near[...] + transpose_product(rows, mixed(u_far[...], slopes, head[...]))


def down_product(top, bottom, u_all, head, near):
    width, depth = near.shape
    tile = width // 2
    h = top.shape[0]
    piece = pl.BlockSpec((h, tile), lambda i: (0, i))
    slope = pl.BlockSpec((h, 128), lambda i: (0, 6 * tile // 128))
    return pl.pallas_call(
        down_kernel,
        out_shape=jax.ShapeDtypeStruct((width, depth), F32),
        grid=(2,),
        in_specs=[
            piece,
            piece,
            slope,
            slope,
            pl.BlockSpec((2 * h, depth), lambda i: (2, 0)),
            pl.BlockSpec((1, depth), lambda i: (0, 0)),
            pl.BlockSpec((tile, depth), lambda i: (i, 0)),
        ],
        out_specs=pl.BlockSpec((tile, depth), lambda i: (i, 0)),
        compiler_params=params(24),
        name="down_product",
    )(top, bottom, top, bottom, u_all, head, near)


def turn_kernel(core, gate, up, out):
    del core
    step = pl.program_id(0)

    @pl.when(step < 2)
    def _():
        out[...] = gate[...].T

    @pl.when(step >= 2)
    def _():
        out[...] = up[...].T


def turned_columns(core, gate_weight, up_weight):
    depth, width = gate_weight.shape
    tile = width // 4
    return pl.pallas_call(
        turn_kernel,
        out_shape=jax.ShapeDtypeStruct((width, depth), BF),
        grid_spec=pltpu.PrefetchScalarGridSpec(
            num_scalar_prefetch=1,
            grid=(4,),
            in_specs=[
                pl.BlockSpec((depth, tile), lambda i, s: (0, 2 * s[0] + jnp.minimum(i, 1))),
                pl.BlockSpec((depth, tile), lambda i, s: (0, 2 * s[0] + jnp.maximum(i - 2, 0))),
            ],
            out_specs=pl.BlockSpec((tile, depth), lambda i, s: (i, 0)),
        ),
        compiler_params=params(16),
        name="turned_columns",
    )(core[None], gate_weight, up_weight)


def input_kernel(source, top, bottom, weight, near, own_out, other_out, total):
    step = pl.program_id(0)
    n = near.shape[0] // 3
    h = n // 2

    @pl.when(step == 0)
    def _():
        total[: 2 * n] = near[: 2 * n]
        total[2 * n : 3 * n] = jnp.zeros((n, total.shape[1]), F32)
        total[3 * n :] = near[2 * n :]

    total[2 * n : 2 * n + h] += product(top[...], weight[...])
    total[2 * n + h : 3 * n] += product(bottom[...], weight[...])

    @pl.when(step == pl.num_programs(0) - 1)
    def _():
        m = n // 4
        for i in range(8):
            own_out[i * m : (i + 1) * m] = total[pl.ds(pl.multiple_of(source[i] * m, m), m)]
            other_out[i * m : (i + 1) * m] = total[
                pl.ds(pl.multiple_of(source[8 + i] * m, m), m)
            ].astype(BF)


def input_product(source, top, bottom, turned_weight, near):
    depth = turned_weight.shape[1]
    tile = turned_weight.shape[0] // 4
    h = top.shape[0]
    return pl.pallas_call(
        input_kernel,
        out_shape=[
            jax.ShapeDtypeStruct((4 * h, depth), F32),
            jax.ShapeDtypeStruct((4 * h, depth), BF),
        ],
        grid_spec=pltpu.PrefetchScalarGridSpec(
            num_scalar_prefetch=1,
            grid=(4,),
            in_specs=[pl.BlockSpec((h, tile), lambda i, s: (0, i + 2))] * 2
            + [
                pl.BlockSpec((tile, depth), lambda i, s: (i, 0)),
                pl.BlockSpec((6 * h, depth), lambda i, s: (0, 0)),
            ],
            out_specs=[pl.BlockSpec((4 * h, depth), lambda i, s: (0, 0))] * 2,
            scratch_shapes=[pltpu.VMEM((8 * h, depth), F32)],
        ),
        compiler_params=params(24),
        name="input_product",
    )(source, top, bottom, turned_weight, near)


def weight_kernel(core, top, bottom, turned_inputs, near, gate_out, up_out, send_out):
    step = pl.program_id(0)
    n = gate_out.shape[0]
    h = top.shape[0]
    piece = joined((top, bottom))

    def product_of(first):
        rows = pl.ds(pl.multiple_of(first, n), n)
        return near[rows, :] + product(turned_inputs[rows, 4 * h : 6 * h], piece)

    def keep(out):
        out[...] = product_of(core[0] * n)

    pl.when(step < 2)(lambda: keep(gate_out))
    pl.when(step >= 2)(lambda: keep(up_out))
    send_out[...] = product_of((1 - core[0]) * n).astype(BF)


def weight_product(core, top, bottom, turned_inputs, near):
    depth, width = near.shape
    tile = width // 4
    h = top.shape[0]
    rows = depth // 2
    return pl.pallas_call(
        weight_kernel,
        out_shape=[
            jax.ShapeDtypeStruct((rows, width), F32),
            jax.ShapeDtypeStruct((rows, width), F32),
            jax.ShapeDtypeStruct((rows, width), BF),
        ],
        grid_spec=pltpu.PrefetchScalarGridSpec(
            num_scalar_prefetch=1,
            grid=(4,),
            in_specs=[pl.BlockSpec((h, tile), lambda i, s: (0, i + 2))] * 2
            + [
                pl.BlockSpec(turned_inputs.shape, lambda i, s: (0, 0)),
                pl.BlockSpec((depth, tile), lambda i, s: (0, i)),
            ],
            out_specs=[
                pl.BlockSpec((rows, tile), lambda i, s: (0, 2 * s[0] + jnp.minimum(i, 1))),
                pl.BlockSpec((rows, tile), lambda i, s: (0, 2 * s[0] + jnp.maximum(i - 2, 0))),
                pl.BlockSpec((rows, tile), lambda i, s: (0, i)),
            ],
        ),
        compiler_params=params(24),
        name="weight_product",
    )(core[None], top, bottom, turned_inputs, near)


def fill_kernel(core, gate_part, up_part, gate_in, up_in, gate_out, up_out):
    del core, gate_in, up_in
    gate_out[...] = gate_part[...].astype(F32)
    up_out[...] = up_part[...].astype(F32)


def fill_columns(core, other, gate_grad, up_grad):
    rows, width = gate_grad.shape
    tile = width // 4
    part = lambda first: pl.BlockSpec((rows, tile), lambda i, s: (0, first + i))
    target = pl.BlockSpec((rows, tile), lambda i, s: (0, 2 - 2 * s[0] + i))
    return pl.pallas_call(
        fill_kernel,
        out_shape=[jax.ShapeDtypeStruct((rows, width), F32)] * 2,
        grid_spec=pltpu.PrefetchScalarGridSpec(
            num_scalar_prefetch=1,
            grid=(2,),
            in_specs=[part(0), part(2)] + [pl.BlockSpec(memory_space=pl.ANY)] * 2,
            out_specs=[target] * 2,
        ),
        input_output_aliases={3: 0, 4: 1},
        compiler_params=params(16),
        name="fill_columns",
    )(core[None], other, other, gate_grad, up_grad)


def add_halves(direct, added, arrived, top_added):
    h, width = direct.shape
    if direct.dtype == F32:
        added = added + arrived.astype(F32)
        both = (added, direct) if top_added else (direct, added)
        return jnp.concatenate(both, 0).astype(BF)
    tile = (width - 128) // 6

    def kernel(direct_ref, added_ref, arrived_ref, out_ref):
        at = 0 if top_added else h
        out_ref[at : at + h] = (added_ref[...] + arrived_ref[...].astype(F32)).astype(BF)
        out_ref[h - at : 2 * h - at] = direct_ref[...].astype(BF)

    return pl.pallas_call(
        kernel,
        out_shape=jax.ShapeDtypeStruct((2 * h, width), BF),
        grid=(7,),
        in_specs=[pl.BlockSpec((h, tile), lambda i: (0, i))] * 3,
        out_specs=pl.BlockSpec((2 * h, tile), lambda i: (0, i)),
        compiler_params=params(16),
        name="add_halves",
    )(direct, added, arrived)


def ring_reduce(far, direct, added, own, ring):
    up, down = move(far[0], ring[1]), move(far[1], ring[3])
    up, down, *held = together(up, down, *direct, *added, *own)
    direct, added, own = held[:2], held[2:4], held[4:]
    below = move(add_halves(direct[0], added[0], up, True), ring[1])
    above = move(add_halves(direct[1], added[1], down, False), ring[3])
    h = own[0].shape[0]
    top = own[0] + below[:h].astype(F32) + above[:h].astype(F32)
    bottom = own[1] + below[h:].astype(F32) + above[h:].astype(F32)
    return top, bottom


def halves(value):
    h = value.shape[0] // 2
    return value[:h], value[h:]


def ring_start(top, bottom, ring):
    ahead_top, behind_bottom = move(top, ring[3]), move(bottom, ring[1])
    ahead_bottom, behind_top = move(bottom, ring[3]), move(top, ring[1])
    return ahead_top, ahead_bottom, behind_top, behind_bottom


def ring_pass(arrived, ring):
    return move(arrived[0], ring[3]), move(arrived[3], ring[1])


def per_device(
    inputs, gate_weight, up_weight, down_weight, reward_head, upstream, labels, label_mask
):
    tokens, depth = inputs.shape
    half = gate_weight.shape[1] // 2
    core = lax.axis_index("dp")
    row = lax.axis_index("row")
    z = lax.axis_index("col")
    y, x = row // SIDE, row % SIDE
    turn = (x + 4 - z) % 4
    mine = tokens // 2
    total = tokens * 8
    head_value = reward_head.astype(F32)
    all_weights = (gate_weight, up_weight, down_weight)

    def around_z(value):
        return [value] + [move(value, AHEAD[4 - s]) for s in (1, 2, 3)]

    def both_cores(own, axis):
        other = move(own, OTHER)
        shape = own.shape[:axis] + (4, 1, tokens) + own.shape[axis + 1 :]
        own, other = own.reshape(shape), other.reshape(shape)
        return jnp.where(
            core == 0,
            jnp.concatenate([own, other], axis + 1),
            jnp.concatenate([other, own], axis + 1),
        )

    def ordered(whole):
        whole = lax.dynamic_slice_in_dim(jnp.concatenate([whole, whole], 0), turn, 4, 0)
        whole = lax.dynamic_slice_in_dim(jnp.concatenate([whole, whole], 1), y, 4, 1)
        return jnp.where(core == 0, whole, whole.transpose(1, 0, 2, 3)).reshape(total, depth)

    down_half = lax.dynamic_slice_in_dim(down_weight, core * half, half, 0)
    head_hidden = jnp.dot(down_half.astype(F32), head_value, precision=lax.Precision.HIGHEST)

    x_own, u_own = around_z(inputs), around_z(upstream)
    *x_own, head_hidden = together(*x_own, head_hidden)
    x_whole = both_cores(jnp.concatenate(x_own, 0), 0).reshape(4, 4, mine, depth)
    x_all = ordered(x_whole)
    u_all = ordered(both_cores(jnp.concatenate(u_own, 0), 0).reshape(4, 4, mine, depth))
    per_token = half // mine
    heads = (
        jnp.pad(reward_head[:, None], ((0, 0), (0, 127))),
        jnp.pad(head_hidden.reshape(mine, per_token), ((0, 0), (1, 127 - per_token))),
    )

    far = project(core, x_all, u_all, all_weights, heads, True)
    rest = project(core, x_all, u_all, all_weights, heads, False)
    top, bottom = ring_reduce(far, rest[:2], rest[2:4], rest[4:], FIRST)
    tags = both_cores(jnp.concatenate(around_z(jnp.stack([labels, label_mask])), 1), 1)
    turned_inputs = x_all.T
    turned_weight = turned_columns(core, gate_weight, up_weight)

    first, second = halves(top)
    third, fourth = halves(bottom)
    second, fourth = halves(second), halves(fourth)
    top, bottom = ring_reduce(
        halves(third.astype(BF)),
        (second[1], fourth[0]),
        (second[0], fourth[1]),
        halves(first),
        SECOND,
    )
    sums = jnp.concatenate([top, bottom], 0)

    gate, upper, grad_upstream = (sums[:, i * half : (i + 1) * half] for i in range(3))
    extra = sums[:, 3 * half :]
    own_inputs, head_hidden = extra[:, 0], extra[:, 1 : 1 + per_token].reshape(half)
    own_tags = lax.dynamic_slice_in_dim(
        tags.reshape(2, total), (turn * 4 + y) * mine, mine, 1
    ).astype(F32)
    sigmoid_gate = jax.nn.sigmoid(gate)
    hidden = (gate * sigmoid_gate * upper).astype(BF)

    part = jnp.sum(hidden.astype(F32) * head_hidden[None, :], axis=1)
    part = part + move(part, AHEAD[1]) + move(part, AHEAD[2]) + move(part, AHEAD[3])
    score = own_inputs + part + move(part, OTHER)
    slope = reward_weight * own_tags[1] * (jax.nn.sigmoid(score) - own_tags[0])
    grad_hidden = grad_upstream + slope[:, None] * head_hidden[None, :]
    grad_gate = (grad_hidden * upper * sigmoid_gate * (1.0 + gate * (1.0 - sigmoid_gate))).astype(
        BF
    )
    grad_upper = (grad_hidden * gate * sigmoid_gate).astype(BF)
    slopes = jnp.pad(jnp.stack(parts_of(slope, 3), axis=1), ((0, 0), (0, 125)))
    block = jnp.concatenate([hidden, grad_gate, grad_upper, slopes], axis=1)

    near = ring_start(*halves(block), SECOND)
    far = ring_pass(near, SECOND)
    top = jnp.concatenate([block, *near[:2]], 0)
    bottom = jnp.concatenate([*far, *near[2:]], 0)
    near = ring_start(top, bottom, FIRST)
    far_top, far_bottom = ring_pass(near, FIRST)

    head_row = head_value[None, :]
    near_down, near_input, near_weight = near_products(
        [top, bottom, *near], turned_weight, turned_inputs, u_all, head_row
    )
    far_top, far_bottom, near_down, near_weight, near_input = together(
        far_top, far_bottom, near_down, near_weight, near_input
    )

    spot = jnp.arange(16, dtype=jnp.int32)
    whose = jnp.where(spot < 8, core, 1 - core)
    along_x = (z + (spot // 2) % 4 + 4 - x) % 4
    along_y = (whose * 2 + spot % 2 + 4 - y) % 4
    source = jnp.where(core == 0, along_x * 4 + along_y, along_y * 4 + along_x)
    last = (far_top, far_bottom)
    own_part, other_part = input_product(source, *last, turned_weight, near_input)
    near_weight, own_part = together(near_weight, own_part)
    other_arrived = move(other_part, OTHER)
    gate_grad, up_grad, send = weight_product(core, *last, turned_inputs, near_weight)
    other = move(send, OTHER)
    near_down, other_arrived = together(near_down, other_arrived)
    blocks = jnp.split(own_part + other_arrived.astype(F32), 4, 0)
    input_sum = blocks[0]
    blocks = [t.astype(BF) for t in blocks[1:]]
    *blocks, near_down = together(*blocks, near_down)
    arrived = [move(blocks[s - 1], AHEAD[s]) for s in (1, 2, 3)]
    down_grad = down_product(*last, u_all, head_row, near_down)

    slope_parts = jnp.concatenate(
        [
            p[:, 6 * (half // 2) :]
            for p in (top, bottom, *near[:2], far_top, far_bottom, *near[2:])
        ],
        0,
    )
    slope_all = slope_parts[:, :3].astype(F32).sum(1)
    own_slope = jnp.concatenate(
        [lax.dynamic_slice_in_dim(slope_all, source[i] * mine, mine, 0) for i in range(2)]
    )

    gate_grad, up_grad = fill_columns(core, other, gate_grad, up_grad)
    *arrived, gate_grad, up_grad, down_grad = together(*arrived, gate_grad, up_grad, down_grad)
    for t in arrived:
        input_sum = input_sum + t.astype(F32)
    input_grad = upstream.astype(F32) + own_slope[:, None] * head_value[None, :] + input_sum
    return (gate_grad, up_grad, down_grad, input_grad)


def solution(mesh):
    in_specs = (
        P(("col", "dp"), "row"),
        P("row", "col"),
        P("row", "col"),
        P("col", "row"),
        P("row"),
        P(("col", "dp"), "row"),
        P(("col", "dp")),
        P(("col", "dp")),
    )
    out_specs = (
        P(("row", "dp"), "col"),
        P(("row", "dp"), "col"),
        P(("col", "dp"), "row"),
        P(("col", "dp"), "row"),
    )
    return jax.shard_map(
        per_device, mesh=mesh, in_specs=in_specs, out_specs=out_specs, check_vma=False
    )
```

```python
import jax
import jax.numpy as jnp
from jax import lax
from jax.experimental import pallas as pl
from jax.experimental.pallas import tpu as pltpu
from jax.sharding import PartitionSpec as P

reward_weight = 8.0
BF = jnp.bfloat16
F32 = jnp.float32
AXES = ("row", "col", "dp")
SIDE = 4


def transpose_product(left, right):
    return lax.dot_general(
        left, right, (((0,), (0,)), ((), ())), preferred_element_type=F32
    )


def right_transpose(left, right):
    return lax.dot_general(
        left, right, (((1,), (1,)), ((), ())), preferred_element_type=F32
    )


def product(left, right):
    return jnp.dot(left, right, preferred_element_type=F32)


def flat(y, x, z, c):
    return ((y * SIDE + x) * 4 + z) * 2 + c


def pairs(move):
    found = []
    for y in range(SIDE):
        for x in range(SIDE):
            for z in range(4):
                for c in range(2):
                    found.append((flat(y, x, z, c), flat(*move(y, x, z, c))))
    return found


def step_first(s):
    return pairs(
        lambda y, x, z, c: (y, (x + s) % SIDE, z, c) if c == 0 else ((y + s) % SIDE, x, z, c)
    )


def step_second(s):
    return pairs(
        lambda y, x, z, c: ((y + s) % SIDE, x, z, c) if c == 0 else (y, (x + s) % SIDE, z, c)
    )


FIRST = {s: step_first(s) for s in (1, 2, 3)}
SECOND = {s: step_second(s) for s in (1, 2, 3)}


def move(value, links):
    return lax.ppermute(value, AXES, links)


AHEAD = {s: pairs(lambda y, x, z, c, s=s: (y, x, (z + s) % 4, c)) for s in (1, 2, 3)}
OTHER = pairs(lambda y, x, z, c: (y, x, z, 1 - c))


def together(*values):
    return lax.optimization_barrier(values)


def parts_of(value, n):
    found = []
    for _ in range(n):
        found.append(value.astype(BF))
        value = value - found[-1].astype(F32)
    return found


def params(mib=24):
    return pltpu.CompilerParams(vmem_limit_bytes=mib << 20)


def project(core, x_all, u_all, weights, heads, far):
    total, depth = x_all.shape
    tile = weights[0].shape[1] // 4
    n = total // 4
    h = n // 2
    spread = heads[1].shape[0]
    starts = (0, h) if far else (n + h, 3 * n, n, 3 * n + h, 0, h)
    types = (BF, BF) if far else (BF, BF, F32, F32, F32, F32)

    def kernel(core_ref, x_ref, u_ref, gate_ref, up_ref, down_ref, head_ref, spread_ref, *outs):
        step = pl.program_id(0)

        def run(rows_ref, of):
            for start, out in zip(starts, outs):
                value = of(rows_ref[start : start + h])
                out[:, : value.shape[1]] = value.astype(out.dtype)

        def heads_of(rows):
            return product(rows, head_ref[...]) + jnp.concatenate(
                [spread_ref[...]] * (h // spread), 0
            )

        pl.when(step < 2)(lambda: run(x_ref, lambda rows: product(rows, gate_ref[...])))
        pl.when((step >= 2) & (step < 4))(
            lambda: run(x_ref, lambda rows: product(rows, up_ref[...]))
        )
        pl.when((step >= 4) & (step < 6))(
            lambda: run(u_ref, lambda rows: right_transpose(rows, down_ref[...]))
        )
        pl.when(step == 6)(lambda: run(x_ref, heads_of))

    whole = lambda v: pl.BlockSpec(v.shape, lambda i, s: (0, 0))
    tokens = pl.BlockSpec((n, depth), lambda i, s: (2, 0)) if far else whole(x_all)
    return pl.pallas_call(
        kernel,
        out_shape=[jax.ShapeDtypeStruct((h, 6 * tile + 128), t) for t in types],
        grid_spec=pltpu.PrefetchScalarGridSpec(
            num_scalar_prefetch=1,
            grid=(7,),
            in_specs=[
                tokens,
                tokens,
                pl.BlockSpec((depth, tile), lambda i, s: (0, 2 * s[0] + jnp.minimum(i, 1))),
                pl.BlockSpec((depth, tile), lambda i, s: (0, 2 * s[0] + jnp.clip(i - 2, 0, 1))),
                pl.BlockSpec((tile, depth), lambda i, s: (2 * s[0] + jnp.clip(i - 4, 0, 1), 0)),
                whole(heads[0]),
                whole(heads[1]),
            ],
            out_specs=[pl.BlockSpec((h, tile), lambda i, s: (0, i)) for _ in types],
        ),
        compiler_params=params(),
        name="project_far" if far else "project_rest",
    )(core[None], x_all, u_all, *weights, *heads)


def joined(refs):
    return jnp.concatenate([ref[...] for ref in refs], 0)


def pairs_of(refs):
    return [
        jnp.concatenate([refs[i][...], refs[i + 1][...]], 0) for i in range(0, len(refs), 2)
    ]


def mixed(u_rows, slopes, head):
    slope = (
        slopes[:, 0:1].astype(F32) + slopes[:, 1:2].astype(F32) + slopes[:, 2:3].astype(F32)
    )
    return (u_rows.astype(F32) + slope * head).astype(BF)


def near_kernel(*refs):
    pieces, slopes, refs = pairs_of(refs[:6]), refs[6:12], refs[12:]
    turned_inputs, u_all, head, weight, down_out, input_out, weight_out = refs
    step = pl.program_id(0)
    n = pieces[0].shape[0]
    starts = (0, n, 3 * n)

    @pl.when(step == 0)
    def _():
        input_out[...] = jnp.zeros_like(input_out)

    @pl.when(step < 2)
    def _():
        found = None
        for piece, slope, at in zip(pieces, pairs_of(slopes), starts):
            term = transpose_product(piece, mixed(u_all[at : at + n], slope, head[...]))
            found = term if found is None else found + term
        down_out[...] = found

    @pl.when(step >= 2)
    def _():
        found = None
        for i, piece in enumerate(pieces):
            input_out[i * n : (i + 1) * n] += product(piece, weight[...])
            term = product(turned_inputs[:, starts[i] : starts[i] + n], piece)
            found = term if found is None else found + term
        weight_out[...] = found


def near_products(pieces, turned_weight, turned_inputs, u_all, head):
    depth, total = turned_inputs.shape
    tile = turned_weight.shape[0] // 4
    h = pieces[0].shape[0]
    n = 2 * h
    return pl.pallas_call(
        near_kernel,
        out_shape=[
            jax.ShapeDtypeStruct((2 * tile, depth), F32),
            jax.ShapeDtypeStruct((3 * n, depth), F32),
            jax.ShapeDtypeStruct((depth, 4 * tile), F32),
        ],
        grid_spec=pl.GridSpec(
            grid=(6,),
            in_specs=[pl.BlockSpec((h, tile), lambda i: (0, i))] * 6
            + [pl.BlockSpec((h, 128), lambda i: (0, 6 * tile // 128))] * 6
            + [
                pl.BlockSpec((depth, total), lambda i: (0, 0)),
                pl.BlockSpec((total, depth), lambda i: (0, 0)),
                pl.BlockSpec((1, depth), lambda i: (0, 0)),
                pl.BlockSpec((tile, depth), lambda i: (jnp.maximum(i - 2, 0), 0)),
            ],
            out_specs=[
                pl.BlockSpec((tile, depth), lambda i: (jnp.minimum(i, 1), 0)),
                pl.BlockSpec((3 * n, depth), lambda i: (0, 0)),
                pl.BlockSpec((depth, tile), lambda i: (0, jnp.maximum(i - 2, 0))),
            ],
        ),
        compiler_params=params(54),
        name="near_products",
    )(*pieces, *pieces, turned_inputs, u_all, head, turned_weight)


def down_kernel(top, bottom, slope_top, slope_bottom, u_far, head, near, out):
    slopes = jnp.concatenate([slope_top[...], slope_bottom[...]], 0)
    rows = jnp.concatenate([top[...], bottom[...]], 0)
    out[...] = near[...] + transpose_product(rows, mixed(u_far[...], slopes, head[...]))


def down_product(top, bottom, u_all, head, near):
    width, depth = near.shape
    tile = width // 2
    h = top.shape[0]
    piece = pl.BlockSpec((h, tile), lambda i: (0, i))
    slope = pl.BlockSpec((h, 128), lambda i: (0, 6 * tile // 128))
    return pl.pallas_call(
        down_kernel,
        out_shape=jax.ShapeDtypeStruct((width, depth), F32),
        grid=(2,),
        in_specs=[
            piece,
            piece,
            slope,
            slope,
            pl.BlockSpec((2 * h, depth), lambda i: (2, 0)),
            pl.BlockSpec((1, depth), lambda i: (0, 0)),
            pl.BlockSpec((tile, depth), lambda i: (i, 0)),
        ],
        out_specs=pl.BlockSpec((tile, depth), lambda i: (i, 0)),
        compiler_params=params(24),
        name="down_product",
    )(top, bottom, top, bottom, u_all, head, near)


def turn_kernel(core, gate, up, out):
    del core
    step = pl.program_id(0)

    @pl.when(step < 2)
    def _():
        out[...] = gate[...].T

    @pl.when(step >= 2)
    def _():
        out[...] = up[...].T


def turned_columns(core, gate_weight, up_weight):
    depth, width = gate_weight.shape
    tile = width // 4
    return pl.pallas_call(
        turn_kernel,
        out_shape=jax.ShapeDtypeStruct((width, depth), BF),
        grid_spec=pltpu.PrefetchScalarGridSpec(
            num_scalar_prefetch=1,
            grid=(4,),
            in_specs=[
                pl.BlockSpec((depth, tile), lambda i, s: (0, 2 * s[0] + jnp.minimum(i, 1))),
                pl.BlockSpec((depth, tile), lambda i, s: (0, 2 * s[0] + jnp.maximum(i - 2, 0))),
            ],
            out_specs=pl.BlockSpec((tile, depth), lambda i, s: (i, 0)),
        ),
        compiler_params=params(16),
        name="turned_columns",
    )(core[None], gate_weight, up_weight)


def input_kernel(source, top, bottom, weight, near, own_out, other_out, total):
    step = pl.program_id(0)
    n = near.shape[0] // 3
    h = n // 2

    @pl.when(step == 0)
    def _():
        total[: 2 * n] = near[: 2 * n]
        total[2 * n : 3 * n] = jnp.zeros((n, total.shape[1]), F32)
        total[3 * n :] = near[2 * n :]

    total[2 * n : 2 * n + h] += product(top[...], weight[...])
    total[2 * n + h : 3 * n] += product(bottom[...], weight[...])

    @pl.when(step == pl.num_programs(0) - 1)
    def _():
        m = n // 4
        for i in range(8):
            own_out[i * m : (i + 1) * m] = total[pl.ds(pl.multiple_of(source[i] * m, m), m)]
            other_out[i * m : (i + 1) * m] = total[
                pl.ds(pl.multiple_of(source[8 + i] * m, m), m)
            ].astype(BF)


def input_product(source, top, bottom, turned_weight, near):
    depth = turned_weight.shape[1]
    tile = turned_weight.shape[0] // 4
    h = top.shape[0]
    return pl.pallas_call(
        input_kernel,
        out_shape=[
            jax.ShapeDtypeStruct((4 * h, depth), F32),
            jax.ShapeDtypeStruct((4 * h, depth), BF),
        ],
        grid_spec=pltpu.PrefetchScalarGridSpec(
            num_scalar_prefetch=1,
            grid=(4,),
            in_specs=[pl.BlockSpec((h, tile), lambda i, s: (0, i + 2))] * 2
            + [
                pl.BlockSpec((tile, depth), lambda i, s: (i, 0)),
                pl.BlockSpec((6 * h, depth), lambda i, s: (0, 0)),
            ],
            out_specs=[pl.BlockSpec((4 * h, depth), lambda i, s: (0, 0))] * 2,
            scratch_shapes=[pltpu.VMEM((8 * h, depth), F32)],
        ),
        compiler_params=params(54),
        name="input_product",
    )(source, top, bottom, turned_weight, near)


def weight_kernel(core, top, bottom, turned_inputs, near, gate_out, up_out, send_out):
    step = pl.program_id(0)
    n = gate_out.shape[0]
    h = top.shape[0]
    piece = joined((top, bottom))

    def product_of(first):
        rows = pl.ds(pl.multiple_of(first, n), n)
        return near[rows, :] + product(turned_inputs[rows, 4 * h : 6 * h], piece)

    def keep(out):
        out[...] = product_of(core[0] * n)

    pl.when(step < 2)(lambda: keep(gate_out))
    pl.when(step >= 2)(lambda: keep(up_out))
    send_out[...] = product_of((1 - core[0]) * n).astype(BF)


def weight_product(core, top, bottom, turned_inputs, near):
    depth, width = near.shape
    tile = width // 4
    h = top.shape[0]
    rows = depth // 2
    return pl.pallas_call(
        weight_kernel,
        out_shape=[
            jax.ShapeDtypeStruct((rows, width), F32),
            jax.ShapeDtypeStruct((rows, width), F32),
            jax.ShapeDtypeStruct((rows, width), BF),
        ],
        grid_spec=pltpu.PrefetchScalarGridSpec(
            num_scalar_prefetch=1,
            grid=(4,),
            in_specs=[pl.BlockSpec((h, tile), lambda i, s: (0, i + 2))] * 2
            + [
                pl.BlockSpec(turned_inputs.shape, lambda i, s: (0, 0)),
                pl.BlockSpec((depth, tile), lambda i, s: (0, i)),
            ],
            out_specs=[
                pl.BlockSpec((rows, tile), lambda i, s: (0, 2 * s[0] + jnp.minimum(i, 1))),
                pl.BlockSpec((rows, tile), lambda i, s: (0, 2 * s[0] + jnp.maximum(i - 2, 0))),
                pl.BlockSpec((rows, tile), lambda i, s: (0, i)),
            ],
        ),
        compiler_params=params(54),
        name="weight_product",
    )(core[None], top, bottom, turned_inputs, near)


def fill_kernel(core, gate_part, up_part, gate_in, up_in, gate_out, up_out):
    del core, gate_in, up_in
    gate_out[...] = gate_part[...].astype(F32)
    up_out[...] = up_part[...].astype(F32)


def fill_columns(core, other, gate_grad, up_grad):
    rows, width = gate_grad.shape
    tile = width // 4
    part = lambda first: pl.BlockSpec((rows, tile), lambda i, s: (0, first + i))
    target = pl.BlockSpec((rows, tile), lambda i, s: (0, 2 - 2 * s[0] + i))
    return pl.pallas_call(
        fill_kernel,
        out_shape=[jax.ShapeDtypeStruct((rows, width), F32)] * 2,
        grid_spec=pltpu.PrefetchScalarGridSpec(
            num_scalar_prefetch=1,
            grid=(2,),
            in_specs=[part(0), part(2)] + [pl.BlockSpec(memory_space=pl.ANY)] * 2,
            out_specs=[target] * 2,
        ),
        input_output_aliases={3: 0, 4: 1},
        compiler_params=params(16),
        name="fill_columns",
    )(core[None], other, other, gate_grad, up_grad)


def add_halves(direct, added, arrived, top_added):
    h, width = direct.shape
    if direct.dtype == F32:
        added = added + arrived.astype(F32)
        both = (added, direct) if top_added else (direct, added)
        return jnp.concatenate(both, 0).astype(BF)
    tile = (width - 128) // 6

    def kernel(direct_ref, added_ref, arrived_ref, out_ref):
        at = 0 if top_added else h
        out_ref[at : at + h] = (added_ref[...] + arrived_ref[...].astype(F32)).astype(BF)
        out_ref[h - at : 2 * h - at] = direct_ref[...].astype(BF)

    return pl.pallas_call(
        kernel,
        out_shape=jax.ShapeDtypeStruct((2 * h, width), BF),
        grid=(7,),
        in_specs=[pl.BlockSpec((h, tile), lambda i: (0, i))] * 3,
        out_specs=pl.BlockSpec((2 * h, tile), lambda i: (0, i)),
        compiler_params=params(16),
        name="add_halves",
    )(direct, added, arrived)


def ring_reduce(far, direct, added, own, ring):
    up, down = move(far[0], ring[1]), move(far[1], ring[3])
    up, down, *held = together(up, down, *direct, *added, *own)
    direct, added, own = held[:2], held[2:4], held[4:]
    below = move(add_halves(direct[0], added[0], up, True), ring[1])
    above = move(add_halves(direct[1], added[1], down, False), ring[3])
    h = own[0].shape[0]
    top = own[0] + below[:h].astype(F32) + above[:h].astype(F32)
    bottom = own[1] + below[h:].astype(F32) + above[h:].astype(F32)
    return top, bottom


def halves(value):
    h = value.shape[0] // 2
    return value[:h], value[h:]


def ring_start(top, bottom, ring):
    ahead_top, behind_bottom = move(top, ring[3]), move(bottom, ring[1])
    ahead_bottom, behind_top = move(bottom, ring[3]), move(top, ring[1])
    return ahead_top, ahead_bottom, behind_top, behind_bottom


def ring_pass(arrived, ring):
    return move(arrived[0], ring[3]), move(arrived[3], ring[1])


def per_device(
    inputs, gate_weight, up_weight, down_weight, reward_head, upstream, labels, label_mask
):
    tokens, depth = inputs.shape
    half = gate_weight.shape[1] // 2
    core = lax.axis_index("dp")
    row = lax.axis_index("row")
    z = lax.axis_index("col")
    y, x = row // SIDE, row % SIDE
    turn = (x + 4 - z) % 4
    mine = tokens // 2
    total = tokens * 8
    head_value = reward_head.astype(F32)
    all_weights = (gate_weight, up_weight, down_weight)

    def around_z(value):
        return [value] + [move(value, AHEAD[4 - s]) for s in (1, 2, 3)]

    def both_cores(own, axis):
        other = move(own, OTHER)
        shape = own.shape[:axis] + (4, 1, tokens) + own.shape[axis + 1 :]
        own, other = own.reshape(shape), other.reshape(shape)
        return jnp.where(
            core == 0,
            jnp.concatenate([own, other], axis + 1),
            jnp.concatenate([other, own], axis + 1),
        )

    def ordered(whole):
        whole = lax.dynamic_slice_in_dim(jnp.concatenate([whole, whole], 0), turn, 4, 0)
        whole = lax.dynamic_slice_in_dim(jnp.concatenate([whole, whole], 1), y, 4, 1)
        return jnp.where(core == 0, whole, whole.transpose(1, 0, 2, 3)).reshape(total, depth)

    down_half = lax.dynamic_slice_in_dim(down_weight, core * half, half, 0)
    head_hidden = jnp.dot(down_half.astype(F32), head_value, precision=lax.Precision.HIGHEST)

    x_own, u_own = around_z(inputs), around_z(upstream)
    *x_own, head_hidden = together(*x_own, head_hidden)
    x_whole = both_cores(jnp.concatenate(x_own, 0), 0).reshape(4, 4, mine, depth)
    x_all = ordered(x_whole)
    u_all = ordered(both_cores(jnp.concatenate(u_own, 0), 0).reshape(4, 4, mine, depth))
    per_token = half // mine
    heads = (
        jnp.pad(reward_head[:, None], ((0, 0), (0, 127))),
        jnp.pad(head_hidden.reshape(mine, per_token), ((0, 0), (1, 127 - per_token))),
    )

    far = project(core, x_all, u_all, all_weights, heads, True)
    rest = project(core, x_all, u_all, all_weights, heads, False)
    top, bottom = ring_reduce(far, rest[:2], rest[2:4], rest[4:], FIRST)
    tags = both_cores(jnp.concatenate(around_z(jnp.stack([labels, label_mask])), 1), 1)
    turned_inputs = x_all.T
    turned_weight = turned_columns(core, gate_weight, up_weight)

    first, second = halves(top)
    third, fourth = halves(bottom)
    second, fourth = halves(second), halves(fourth)
    top, bottom = ring_reduce(
        halves(third.astype(BF)),
        (second[1], fourth[0]),
        (second[0], fourth[1]),
        halves(first),
        SECOND,
    )
    sums = jnp.concatenate([top, bottom], 0)

    gate, upper, grad_upstream = (sums[:, i * half : (i + 1) * half] for i in range(3))
    extra = sums[:, 3 * half :]
    own_inputs, head_hidden = extra[:, 0], extra[:, 1 : 1 + per_token].reshape(half)
    own_tags = lax.dynamic_slice_in_dim(
        tags.reshape(2, total), (turn * 4 + y) * mine, mine, 1
    ).astype(F32)
    sigmoid_gate = jax.nn.sigmoid(gate)
    hidden = (gate * sigmoid_gate * upper).astype(BF)

    part = jnp.sum(hidden.astype(F32) * head_hidden[None, :], axis=1)
    part = part + move(part, AHEAD[1]) + move(part, AHEAD[2]) + move(part, AHEAD[3])
    score = own_inputs + part + move(part, OTHER)
    slope = reward_weight * own_tags[1] * (jax.nn.sigmoid(score) - own_tags[0])
    grad_hidden = grad_upstream + slope[:, None] * head_hidden[None, :]
    grad_gate = (grad_hidden * upper * sigmoid_gate * (1.0 + gate * (1.0 - sigmoid_gate))).astype(
        BF
    )
    grad_upper = (grad_hidden * gate * sigmoid_gate).astype(BF)
    slopes = jnp.pad(jnp.stack(parts_of(slope, 3), axis=1), ((0, 0), (0, 125)))
    block = jnp.concatenate([hidden, grad_gate, grad_upper, slopes], axis=1)

    near = ring_start(*halves(block), SECOND)
    far = ring_pass(near, SECOND)
    top = jnp.concatenate([block, *near[:2]], 0)
    bottom = jnp.concatenate([*far, *near[2:]], 0)
    near = ring_start(top, bottom, FIRST)
    far_top, far_bottom = ring_pass(near, FIRST)

    head_row = head_value[None, :]
    near_down, near_input, near_weight = near_products(
        [top, bottom, *near], turned_weight, turned_inputs, u_all, head_row
    )
    far_top, far_bottom, near_down, near_weight, near_input = together(
        far_top, far_bottom, near_down, near_weight, near_input
    )

    spot = jnp.arange(16, dtype=jnp.int32)
    whose = jnp.where(spot < 8, core, 1 - core)
    along_x = (z + (spot // 2) % 4 + 4 - x) % 4
    along_y = (whose * 2 + spot % 2 + 4 - y) % 4
    source = jnp.where(core == 0, along_x * 4 + along_y, along_y * 4 + along_x)
    last = (far_top, far_bottom)
    own_part, other_part = input_product(source, *last, turned_weight, near_input)
    near_weight, own_part = together(near_weight, own_part)
    other_arrived = move(other_part, OTHER)
    gate_grad, up_grad, send = weight_product(core, *last, turned_inputs, near_weight)
    other = move(send, OTHER)
    near_down, other_arrived = together(near_down, other_arrived)
    blocks = jnp.split(own_part + other_arrived.astype(F32), 4, 0)
    input_sum = blocks[0]
    blocks = [t.astype(BF) for t in blocks[1:]]
    *blocks, near_down = together(*blocks, near_down)
    arrived = [move(blocks[s - 1], AHEAD[s]) for s in (1, 2, 3)]
    down_grad = down_product(*last, u_all, head_row, near_down)

    slope_parts = jnp.concatenate(
        [
            p[:, 6 * (half // 2) :]
            for p in (top, bottom, *near[:2], far_top, far_bottom, *near[2:])
        ],
        0,
    )
    slope_all = slope_parts[:, :3].astype(F32).sum(1)
    own_slope = jnp.concatenate(
        [lax.dynamic_slice_in_dim(slope_all, source[i] * mine, mine, 0) for i in range(2)]
    )

    gate_grad, up_grad = fill_columns(core, other, gate_grad, up_grad)
    *arrived, gate_grad, up_grad, down_grad = together(*arrived, gate_grad, up_grad, down_grad)
    for t in arrived:
        input_sum = input_sum + t.astype(F32)
    input_grad = upstream.astype(F32) + own_slope[:, None] * head_value[None, :] + input_sum
    return (gate_grad, up_grad, down_grad, input_grad)


def solution(mesh):
    in_specs = (
        P(("col", "dp"), "row"),
        P("row", "col"),
        P("row", "col"),
        P("col", "row"),
        P("row"),
        P(("col", "dp"), "row"),
        P(("col", "dp")),
        P(("col", "dp")),
    )
    out_specs = (
        P(("row", "dp"), "col"),
        P(("row", "dp"), "col"),
        P(("col", "dp"), "row"),
        P(("col", "dp"), "row"),
    )
    return jax.shard_map(
        per_device, mesh=mesh, in_specs=in_specs, out_specs=out_specs, check_vma=False
    )
```
